256 devices in a mesh: sib: 8 (over z), ctx: 8 (over x, core), head: 4 (over y).
Axes of the slice: x: 4, y: 4, z: 8, core: 2. Of those that a mesh axis runs over, the one named last changes fastest.
Arguments:
- queries: bfloat16 [8, 4096, 4, 1536], P('sib', 'ctx', 'head'), may hold values from -8 to 8
- suffix_kv: bfloat16 [8, 4096, 4, 320], P('sib', 'ctx', 'head'), may hold values from -6 to 6
- prefix_kv: bfloat16 [131072, 4, 320], P(('sib', 'ctx'), 'head'), may hold values from -6 to 6
- pooling: float32 [2, 64], replicated, may hold values from 0.03 to 0.3
- gate_logits: float32 [8, 4096, 4, 24], P('sib', 'ctx', 'head'), may hold values from -6 to 6
- selected: int32 [8, 64, 4, 16], P('sib', 'ctx', 'head'), may hold values from 0 to 2047, as said below
- lengths: int32 [8], P('sib'), may hold values from 512 to 4096, as said below
- w_out: bfloat16 [4096, 2560], P('head'), may hold values from -0.375 to 0.375
Outputs:
- layer_out: bfloat16 [8, 4096, 2560], P('sib', ('ctx', 'head'))
The draws below stay inside these ranges and needn't reach their ends.
Inputs may be any that keep to these rules, and one draw needn't show every extreme that they name: For each sibling and group, the 16 indices of a query block are distinct, and the query blocks of one index of ctx (8 aligned query blocks) select together at most 3 blocks, counted with repeats, among any aligned range of 32 prefix blocks; some range is selected exactly 3 times in every such run. `lengths`: some sibling has the full length 4096 and some the length 512.
All inputs are finite; a program needn't handle non-finite values.
Results may differ from the reference program's by a relative error of at most 0.0096.
Values may be sent and summed in bfloat16 or wider, within the bound.
A program may use at most 192 MiB of HBM per device.

```python
import math
import jax
import jax.numpy as jnp
from jax import lax

DK = 192
DV = 128
HQ = 8
DM = 2560
BLK = 64
TOPK = 16
W = 512
SUF_DEV = 512
GROUPS = 4
SIBLINGS = 8
SUF = 4096
PREFIX = 131072
QB_DEV = 8
QBLK = 64
BPD = 32
NCMP = 2048
OWNERS = 64
CAP = 3


def draw_kv_rows(key, salt_value, lead_shape):
    subkey = jax.random.fold_in(key, salt_value)
    key_part, value_part = jax.random.split(subkey, 2)
    full_shape = lead_shape + (GROUPS,)
    key_rows = jnp.clip(jax.random.normal(key_part, full_shape + (DK,)), -4.0, 4.0)
    value_rows = jnp.clip(jax.random.normal(value_part, full_shape + (DV,)), -4.0, 4.0)
    return jnp.concatenate([key_rows, value_rows], axis=-1).astype(jnp.bfloat16)


def draw_prefix_kv(key, part):
    return draw_kv_rows(key, 11, (PREFIX,))


def draw_suffix_kv(key, part):
    return draw_kv_rows(key, 12, (SIBLINGS, SUF))


def draw_queries(key, part):
    full_shape = (SIBLINGS, SUF, GROUPS, HQ * DK)
    noise_key = jax.random.fold_in(jax.random.fold_in(key, 13), 0)
    values = 2.0 * jnp.clip(jax.random.normal(noise_key, full_shape), -4.0, 4.0)
    return values.astype(jnp.bfloat16)


def draw_selected(key, part):
    ctx_devices = QBLK // QB_DEV
    slot_total = QB_DEV * TOPK
    pool_total = OWNERS * CAP

    def single_draw(subkey):
        first_key, order_key, local_key = jax.random.split(subkey, 3)
        first_owner = jax.random.randint(first_key, (), 0, OWNERS)
        copy_index = jnp.arange(pool_total, dtype=jnp.int32)
        owner_all = copy_index // CAP
        order_scores = jax.random.permutation(order_key, pool_total).astype(jnp.int32)
        order_scores = jnp.where(owner_all == first_owner, copy_index % CAP - CAP, order_scores)
        sorted_pos = jnp.argsort(order_scores, stable=True)
        slot_owner = owner_all[sorted_pos[:slot_total]]
        owner_match = (slot_owner[:, None] == jnp.arange(OWNERS, dtype=jnp.int32)[None, :]).astype(jnp.int32)
        slot_rank = jnp.sum((jnp.cumsum(owner_match, axis=0) - 1) * owner_match, axis=1)
        local_perm = jax.vmap(lambda owner_key: jax.random.permutation(owner_key, BPD))(jax.random.split(local_key, OWNERS))
        slot_local = local_perm[slot_owner, slot_rank].astype(jnp.int32)
        return (slot_owner * BPD + slot_local).astype(jnp.int32).reshape(QB_DEV, TOPK)
    subkeys = jax.random.split(jax.random.fold_in(key, 14), SIBLINGS * ctx_devices * GROUPS)
    drawn = jax.vmap(single_draw)(subkeys)
    drawn = drawn.reshape(SIBLINGS, ctx_devices, GROUPS, QB_DEV, TOPK)
    return jnp.transpose(drawn, (0, 1, 3, 2, 4)).reshape(SIBLINGS, QBLK, GROUPS, TOPK)


def draw_lengths(key, part):
    base_key, perm_key = jax.random.split(jax.random.fold_in(key, 15))
    drawn = jax.random.randint(base_key, (SIBLINGS,), SUF // 8, SUF + 1)
    order_perm = jax.random.permutation(perm_key, SIBLINGS)
    drawn = drawn.at[order_perm[0]].set(SUF)
    drawn = drawn.at[order_perm[1]].set(SUF // 8)
    return drawn.astype(jnp.int32)


def steps_of(key, extent, shards, smallest, largest):
    def one(dim, blocks):
        steps = jax.random.uniform(jax.random.fold_in(jax.random.fold_in(key, 6), dim), (blocks,), jnp.float32, smallest / len(shards), largest / len(shards))
        return jnp.repeat(jnp.exp(steps), extent[dim] // blocks).reshape((-1,) + (1,) * (len(extent) - dim - 1))

    level = one(*shards[0])
    for cut in shards[1:]:
        level = level * one(*cut)
    return level


def scatter_about(stream_key, shape, deviation, limit, cuts=(), kind=jnp.bfloat16):
    values = jax.random.normal(stream_key, shape, jnp.float32) * deviation
    if len(cuts) > 0:
        values = steps_of(stream_key, shape, cuts, -0.22, 0.18) * values
    return jnp.clip(values, min=-limit, max=limit).astype(kind)


def setup_inputs(seed: int = 0) -> dict:
    splits = jax.random.split(jax.random.key(seed), 9)
    return {
        "queries": draw_queries(jax.random.fold_in(splits[8], 71), 0),
        "suffix_kv": draw_suffix_kv(jax.random.fold_in(splits[8], 71), 0),
        "prefix_kv": draw_prefix_kv(jax.random.fold_in(splits[8], 71), 0),
        "pooling": jnp.clip(jnp.exp(jax.random.uniform(splits[3], (2, BLK), jnp.float32, math.log(0.03), math.log(0.3))), 0.03, 0.3),
        "gate_logits": scatter_about(splits[4], (SIBLINGS, SUF, GROUPS, 3 * HQ), 1.5, 6.0, ((0, 8), (1, 8), (2, 4)), jnp.float32),
        "selected": draw_selected(jax.random.fold_in(splits[8], 71), 0),
        "lengths": draw_lengths(jax.random.fold_in(splits[8], 71), 0),
        "w_out": scatter_about(splits[7], (GROUPS * HQ * DV, DM), (HQ * DV // 4) ** -0.5, 0.375, ((0, 4),)),
    }


def softmax_parts(scores):
    row_max = jnp.max(scores, axis=-1, keepdims=True)
    weights = jnp.exp(scores - row_max)
    row_total = jnp.sum(weights, axis=-1, keepdims=True)
    rounded = lax.optimization_barrier(weights.astype(jnp.bfloat16))
    return rounded.astype(jnp.float32), row_total


def compress(group_kv, pooling):
    blocks = group_kv.reshape(-1, BLK, DK + DV).astype(jnp.float32)
    comp_keys = jnp.einsum("bjd,j->bd", blocks[:, :, :DK], pooling[0], precision=lax.Precision.HIGHEST)
    comp_values = jnp.einsum("bjd,j->bd", blocks[:, :, DK:], pooling[1], precision=lax.Precision.HIGHEST)
    return jnp.concatenate([comp_keys, comp_values], axis=-1).astype(jnp.bfloat16)


def reference(queries, suffix_kv, prefix_kv, pooling, gate_logits, selected, lengths, w_out):
    score_scale = DK ** -0.5
    window_reach = -(-W // SUF_DEV)
    group_prefix = jnp.moveaxis(prefix_kv, 1, 0)
    compressed = lax.map(lambda group_kv: compress(group_kv, pooling), group_prefix)
    prefix_blocks = group_prefix.reshape(GROUPS, NCMP, BLK, DK + DV)

    def one_sibling(sib_inputs):
        sib_queries, sib_kv, sib_gates, sib_selected, sib_length = sib_inputs

        def one_group(group_inputs):
            group_queries, group_kv, group_gates, group_selected, group_comp, group_blocks = group_inputs
            padded_kv = jnp.concatenate([jnp.zeros((window_reach * SUF_DEV, DK + DV), group_kv.dtype), group_kv], axis=0)
            comp_float = group_comp.astype(jnp.float32)

            def one_block(block_index):
                row_begin = block_index * SUF_DEV
                query_rows = lax.dynamic_slice_in_dim(group_queries, row_begin, SUF_DEV, 0)
                query_rows = query_rows.reshape(SUF_DEV, HQ, DK).astype(jnp.float32)
                scores = jnp.einsum("rhd,kd->rhk", query_rows, comp_float[:, :DK]) * score_scale
                weights, row_total = softmax_parts(scores)
                comp_out = jnp.einsum("rhk,kd->rhd", weights, comp_float[:, DK:]) / row_total

                block_ids = lax.dynamic_slice_in_dim(group_selected, block_index * QB_DEV, QB_DEV, 0)
                picked = group_blocks[block_ids].reshape(QB_DEV, TOPK * BLK, DK + DV).astype(jnp.float32)
                query_blocks = query_rows.reshape(QB_DEV, BLK, HQ, DK)
                scores = jnp.einsum("qthd,qkd->qhtk", query_blocks, picked[:, :, :DK]) * score_scale
                weights, row_total = softmax_parts(scores)
                sel_out = jnp.einsum("qhtk,qkd->qhtd", weights, picked[:, :, DK:]) / row_total
                sel_out = jnp.transpose(sel_out, (0, 2, 1, 3)).reshape(SUF_DEV, HQ, DV)

                near_kv = lax.dynamic_slice_in_dim(padded_kv, row_begin, (window_reach + 1) * SUF_DEV, 0).astype(jnp.float32)
                query_pos = row_begin + jnp.arange(SUF_DEV, dtype=jnp.int32)
                key_pos = row_begin - window_reach * SUF_DEV + jnp.arange((window_reach + 1) * SUF_DEV, dtype=jnp.int32)
                visible = (key_pos[None, :] <= query_pos[:, None]) & (key_pos[None, :] > query_pos[:, None] - W) & (key_pos[None, :] >= 0)
                scores = jnp.einsum("rhd,kd->rhk", query_rows, near_kv[:, :DK]) * score_scale
                scores = jnp.where(visible[:, None, :], scores, -jnp.inf)
                weights, row_total = softmax_parts(scores)
                win_out = jnp.einsum("rhk,kd->rhd", weights, near_kv[:, DK:]) / row_total

                gate_rows = lax.dynamic_slice_in_dim(group_gates, row_begin, SUF_DEV, 0)
                gate_values = jax.nn.sigmoid(gate_rows.reshape(SUF_DEV, 3, HQ))
                head_out = gate_values[:, 0, :, None] * comp_out + gate_values[:, 1, :, None] * sel_out + gate_values[:, 2, :, None] * win_out
                head_out = jnp.where((query_pos < sib_length)[:, None, None], head_out, 0.0)
                return head_out.astype(jnp.bfloat16).reshape(SUF_DEV, HQ * DV)

            block_outs = lax.map(one_block, jnp.arange(SUF // SUF_DEV, dtype=jnp.int32))
            return block_outs.reshape(SUF, HQ * DV)

        group_outs = lax.map(one_group, (jnp.moveaxis(sib_queries, 1, 0), jnp.moveaxis(sib_kv, 1, 0), jnp.moveaxis(sib_gates, 1, 0), jnp.moveaxis(sib_selected, 1, 0), compressed, prefix_blocks))
        joined = jnp.moveaxis(group_outs, 0, 1).reshape(SUF, GROUPS * HQ * DV)
        return jnp.dot(joined, w_out, preferred_element_type=jnp.float32).astype(jnp.bfloat16)

    return lax.map(one_sibling, (queries, suffix_kv, gate_logits, selected, lengths))
```

```python
import functools

import jax
import jax.numpy as jnp
from jax import lax
from jax.experimental import pallas as pl
from jax.experimental.pallas import tpu as pltpu
from jax.sharding import PartitionSpec as P

DK = 192
DV = 128
KV = DK + DV
HQ = 8
DM = 2560
BLK = 64
W = 512
ROWS = 512
NB = 32
TOPK = 16
QB = ROWS // BLK
NZ = 8
NC = 8
CAP = 3
PAIRS = NB // 2
CHUNK = 4
LANES = 128
TILE = HQ * BLK
SCALE2 = DK ** (-0.5) * 1.4426950408889634
MESH = pl.DeviceIdType.MESH
BF16 = jnp.bfloat16
F32 = jnp.float32


def remote(source, target, send_sem, recv_sem, device):
    return pltpu.make_async_remote_copy(
        src_ref=source,
        dst_ref=target,
        send_sem=send_sem,
        recv_sem=recv_sem,
        device_id=device,
        device_id_type=MESH,
    )


def swap_halves(tile):
    return jnp.concatenate([tile[:, 64:], tile[:, :64]], axis=1)


def layer_kernel(
    pos_ref,
    len_ref,
    q_ref,
    suffix_ref,
    prefix_ref,
    comp_ref,
    request_ref,
    gate_ref,
    out_ref,
    own,
    plus1,
    plus2,
    plus3,
    minus1,
    minus2,
    minus3,
    far,
    outgoing,
    incoming,
    comp_all,
    near,
    asked,
    asked_smem,
    q_raw,
    q_heads,
    mixed,
    sel_kv,
    load_sem,
    misc_sem,
    z_send,
    z_recv,
    x_send,
    x_recv,
    comp_send,
    comp_recv,
    ask_send,
    ask_recv,
    ask_load,
    halo_send,
    halo_recv,
):
    z = lax.axis_index("sib")
    c = lax.axis_index("ctx")
    y = lax.axis_index("head")

    def z_peer(offset):
        return ((z + offset) % NZ, c, y)

    def c_peer(offset):
        return (z, (c + offset) % NC, y)

    barrier = pltpu.get_barrier_semaphore()
    for offset in range(1, NZ):
        pl.semaphore_signal(barrier, inc=1, device_id=z_peer(offset), device_id_type=MESH)
    for offset in range(1, NC):
        pl.semaphore_signal(barrier, inc=1, device_id=c_peer(offset), device_id_type=MESH)

    loads = [
        pltpu.make_async_copy(
            prefix_ref.at[:, pl.ds(pair * LANES, LANES)], own.at[pair], load_sem.at[pair]
        )
        for pair in range(PAIRS)
    ]
    for load in loads:
        load.start()
    q_load = pltpu.make_async_copy(q_ref, q_raw, misc_sem.at[0])
    q_load.start()
    near_load = pltpu.make_async_copy(suffix_ref, near.at[:, pl.ds(ROWS, ROWS)], misc_sem.at[1])
    near_load.start()
    comp_load = pltpu.make_async_copy(comp_ref, comp_all.at[0, 0], misc_sem.at[2])
    comp_load.start()
    ask_self = pltpu.make_async_copy(request_ref.at[0], asked_smem.at[0], ask_load.at[0])
    ask_self.start()
    pl.semaphore_wait(barrier, NZ - 1 + NC - 1)

    def comp_over_z(offset):
        return remote(
            comp_ref,
            comp_all.at[0, NZ - offset],
            comp_send.at[0, offset],
            comp_recv.at[0, NZ - offset],
            z_peer(offset),
        )

    def comp_over_c(offset):
        return remote(
            comp_all.at[0],
            comp_all.at[NC - offset],
            comp_send.at[1, offset],
            comp_recv.at[1, NC - offset],
            c_peer(offset),
        )

    def ask(offset):
        return remote(
            request_ref.at[offset],
            asked.at[NC - offset],
            ask_send.at[offset],
            ask_recv.at[NC - offset],
            c_peer(offset),
        )

    def halo():
        return remote(
            suffix_ref, near.at[:, pl.ds(0, ROWS)], halo_send.at[0], halo_recv.at[0], c_peer(1)
        )

    stages = {1: (own, plus1, plus2, plus3, far), -1: (own, minus1, minus2, minus3, far)}

    def z_chunks(way, step):
        if step < 3:
            return tuple(range(4))
        return (0, 1) if way == 1 else (2, 3)

    def z_copy(way, step, chunk):
        row = 0 if way == 1 else 1
        window = pl.ds(CHUNK * chunk, CHUNK)
        return remote(
            stages[way][step].at[window],
            stages[way][step + 1].at[window],
            z_send.at[row, step, chunk],
            z_recv.at[row, step, chunk],
            z_peer(way),
        )

    def x_copy(plane, offset):
        return remote(
            outgoing.at[pl.ds((plane * NC + offset) * CAP, CAP)],
            incoming.at[pl.ds((plane * NC + NC - offset) * CAP, CAP)],
            x_send.at[plane, offset],
            x_recv.at[plane, NC - offset],
            c_peer(offset),
        )

    left_half = lax.broadcasted_iota(jnp.int32, (KV // 2, LANES), 1) < BLK

    planes = {0: own, 7: plus1, 6: plus2, 5: plus3, 1: minus1, 2: minus2, 3: minus3, 4: far}

    def fill(plane):
        held = planes[plane]

        def one(index, carry):
            offset = index // CAP
            slot = index % CAP
            pair = asked_smem[offset, plane, slot]
            half = asked_smem[offset, plane, CAP + slot]
            tile = held[pair]
            upper = tile[: KV // 2]
            lower = tile[KV // 2 :]
            first = half == 0
            kept_upper = jnp.where(first, upper, swap_halves(upper))
            kept_lower = jnp.where(first, swap_halves(lower), lower)
            outgoing[plane * NC * CAP + index] = jnp.where(left_half, kept_upper, kept_lower)
            return carry

        lax.fori_loop(0, NC * CAP, one, 0)
        base = plane * NC * CAP
        incoming[pl.ds(base, CAP)] = outgoing[pl.ds(base, CAP)]

    def send_plane(plane):
        for offset in (2, 6, 4, 3, 5, 1, 7):
            x_copy(plane, offset).start()

    def forward(step, chunk):
        for way in (1, -1):
            if chunk in z_chunks(way, step):
                z_copy(way, step, chunk).wait_recv()
                if step < 3 and chunk in z_chunks(way, step + 1):
                    z_copy(way, step + 1, chunk).start()

    for offset in (4, 3, 5, 2, 6, 1, 7):
        comp_over_z(offset).start()
    for offset in range(1, NC):
        ask(offset).start()
    halo().start()
    for load in loads:
        load.wait()
    for chunk in range(4):
        for way in (1, -1):
            z_copy(way, 0, chunk).start()

    q_load.wait()
    for head in range(HQ):
        q_heads[head] = q_raw[:, head * DK : (head + 1) * DK]

    for offset in range(1, NC):
        ask(NC - offset).wait_recv()
        pltpu.make_async_copy(asked.at[offset], asked_smem.at[offset], ask_load.at[offset]).start()
    comp_load.wait()
    for offset in range(1, NZ):
        comp_over_z(NZ - offset).wait_recv()
    for offset in (4, 2, 6, 3, 5, 1, 7):
        comp_over_c(offset).start()
    for offset in range(1, NC):
        pltpu.make_async_copy(asked.at[offset], asked_smem.at[offset], ask_load.at[offset]).wait()
    ask_self.wait()
    fill(0)

    def queries_of(block):
        rows = pl.ds(pl.multiple_of(block * BLK, BLK), BLK)
        return q_heads[:, rows, :].reshape(TILE, DK)

    def gate_columns(block):
        rows = pl.ds(pl.multiple_of(block * BLK, BLK), BLK)
        return gate_ref[rows, :]

    def softmax(scores, previous_max=None):
        top = jnp.max(scores, axis=-1, keepdims=True)
        if previous_max is not None:
            top = jnp.maximum(previous_max, top)
        weights = jnp.exp2(scores * SCALE2 - top * SCALE2)
        return top, weights, jnp.sum(weights, axis=-1, keepdims=True)

    nt = (((1,), (1,)), ((), ()))

    near_load.wait()
    halo().wait_recv()

    def window_block(block, carry):
        start = pl.multiple_of((block // 2) * LANES, LANES)
        span = pl.ds(start, W + LANES)
        scores = jnp.dot(queries_of(block), near[:DK, span], preferred_element_type=F32)
        scores = scores.reshape(HQ, BLK, W + LANES)
        row = lax.broadcasted_iota(jnp.int32, (1, BLK, W + LANES), 1) + (block % 2) * BLK
        lane = lax.broadcasted_iota(jnp.int32, (1, BLK, W + LANES), 2)
        reach = jnp.where(c == 0, ROWS - start, 0)
        visible = (lane > row) & (lane <= row + W) & (lane >= reach)
        scores = jnp.where(visible, scores, -jnp.inf).reshape(TILE, W + LANES)
        _, weights, total = softmax(scores)
        result = lax.dot_general(
            weights.astype(BF16), near[DK:, span], nt, preferred_element_type=F32
        )
        result = result / total
        gates = gate_columns(block)
        for head in range(HQ):
            mixed[block, head * BLK : (head + 1) * BLK, :] = (
                result[head * BLK : (head + 1) * BLK]
                * gates[:, 2 * HQ + head : 2 * HQ + head + 1]
            )
        return carry

    window_block(0, 0)
    send_plane(0)

    def window_loop(block, carry):
        window_block(block, carry)

        @pl.when(block == 2)
        def _():
            forward(0, 0)

        @pl.when(block == 4)
        def _():
            forward(0, 1)

        @pl.when(block == 6)
        def _():
            forward(0, 2)

        return carry

    lax.fori_loop(1, QB, window_loop, 0)

    for offset in range(1, NC):
        comp_over_c(NC - offset).wait_recv()

    half_keys = NZ * NC * NB // 2

    def comp_block(block, carry):
        queries = queries_of(block)
        comp_flat = comp_all.reshape(NZ * NC * NB, 3 * LANES)
        top = None
        for part in range(2):
            keys = pl.ds(part * half_keys, half_keys)
            scores = lax.dot_general(
                queries, comp_flat[keys, :DK], nt, preferred_element_type=F32
            )
            new_top, weights, total = softmax(scores, top)
            result = jnp.dot(
                weights.astype(BF16), comp_flat[keys, 2 * LANES :], preferred_element_type=F32
            )
            if part == 0:
                top, all_total, all_result = new_top, total, result
            else:
                decay = jnp.exp2((top - new_top) * SCALE2)
                all_total = all_total * decay + total
                all_result = all_result * decay + result
        result = all_result / all_total
        gates = gate_columns(block)
        for head in range(HQ):
            rows = slice(head * BLK, (head + 1) * BLK)
            mixed[block, rows, :] += result[rows] * gates[:, head : head + 1]
        return carry

    def comp_loop(block, carry):
        comp_block(block, carry)

        @pl.when(block == 0)
        def _():
            forward(0, 3)
            fill(1)
            fill(7)

        @pl.when(block == 1)
        def _():
            send_plane(1)
            send_plane(7)
            forward(1, 0)

        @pl.when(block == 3)
        def _():
            forward(1, 1)

        @pl.when(block == 5)
        def _():
            forward(1, 2)

        return carry

    lax.fori_loop(0, QB, comp_loop, 0)

    forward(1, 3)
    fill(2)
    fill(6)
    forward(2, 0)
    send_plane(2)
    send_plane(6)
    forward(2, 1)
    forward(2, 2)
    forward(2, 3)
    fill(3)
    fill(5)
    forward(3, 0)
    send_plane(3)
    send_plane(5)
    forward(3, 1)
    forward(3, 2)
    forward(3, 3)
    fill(4)
    send_plane(4)
    for plane in (0, 1, 7, 2, 6, 3, 5, 4):
        for offset in range(1, NC):
            x_copy(plane, NC - offset).wait_recv()

    def selected_block(block, carry):
        for pair in range(TOPK // 2):
            first = incoming[pos_ref[block, 2 * pair]]
            second = incoming[pos_ref[block, 2 * pair + 1]]
            lanes = slice(pair * LANES, (pair + 1) * LANES)
            sel_kv[: KV // 2, lanes] = jnp.where(left_half, first, swap_halves(second))
            sel_kv[KV // 2 :, lanes] = jnp.where(left_half, swap_halves(first), second)
        scores = jnp.dot(queries_of(block), sel_kv[:DK, :], preferred_element_type=F32)
        _, weights, total = softmax(scores)
        result = lax.dot_general(
            weights.astype(BF16), sel_kv[DK:, :], nt, preferred_element_type=F32
        )
        result = result / total
        gates = gate_columns(block)
        first_row = pl.multiple_of(block * BLK, BLK)
        inside = (
            lax.broadcasted_iota(jnp.int32, (BLK, DV), 0) + c * ROWS + block * BLK < len_ref[0]
        )
        for head in range(HQ):
            rows = slice(head * BLK, (head + 1) * BLK)
            value = (
                mixed[block, rows, :] + result[rows] * gates[:, HQ + head : HQ + head + 1]
            )
            out_ref[pl.ds(first_row, BLK), head * DV : (head + 1) * DV] = jnp.where(
                inside, value, 0.0
            ).astype(BF16)
        return carry

    lax.fori_loop(0, QB, selected_block, 0)

    for offset in range(1, NZ):
        comp_over_z(offset).wait_send()
    for offset in range(1, NC):
        comp_over_c(offset).wait_send()
        ask(offset).wait_send()
        for plane in range(NZ):
            x_copy(plane, offset).wait_send()
    halo().wait_send()
    for step in range(4):
        for way in (1, -1):
            for chunk in z_chunks(way, step):
                z_copy(way, step, chunk).wait_send()


def attend(pos, length, q_rows, suffix_t, prefix_t, comp, requests, gates):
    anywhere = pl.BlockSpec(memory_space=pl.ANY)
    vmem = pl.BlockSpec(memory_space=pltpu.VMEM)
    smem = pl.BlockSpec(memory_space=pltpu.SMEM)
    plane = pltpu.VMEM((PAIRS, KV, LANES), BF16)
    slots = pltpu.VMEM((NZ * NC * CAP, KV // 2, LANES), BF16)
    dma = pltpu.SemaphoreType.DMA
    return pl.pallas_call(
        layer_kernel,
        name="layer",
        out_shape=jax.ShapeDtypeStruct((ROWS, HQ * DV), BF16),
        in_specs=[smem, smem, anywhere, anywhere, anywhere, anywhere, anywhere, vmem],
        out_specs=vmem,
        scratch_shapes=[plane] * 8
        + [
            slots,
            slots,
            pltpu.VMEM((NC, NZ, NB, 3 * LANES), BF16),
            pltpu.VMEM((KV, 2 * ROWS), BF16),
            pltpu.VMEM((NC, NZ, LANES), jnp.int32),
            pltpu.SMEM((NC, NZ, LANES), jnp.int32),
            pltpu.VMEM((ROWS, HQ * DK), BF16),
            pltpu.VMEM((HQ, ROWS, DK), BF16),
            pltpu.VMEM((QB, TILE, DV), F32),
            pltpu.VMEM((KV, TOPK * BLK), BF16),
            dma((PAIRS,)),
            dma((4,)),
            dma((2, 4, 4)),
            dma((2, 4, 4)),
            dma((NZ, NC)),
            dma((NZ, NC)),
            dma((2, NC)),
            dma((2, NC)),
            dma((NC,)),
            dma((NC,)),
            dma((NC,)),
            dma((1,)),
            dma((1,)),
        ],
        compiler_params=pltpu.CompilerParams(
            collective_id=0, has_side_effects=True, vmem_limit_bytes=60 * 1024 * 1024
        ),
    )(pos, length, q_rows, suffix_t, prefix_t, comp, requests, gates)


def shards(queries, suffix_kv, prefix_kv, pooling, gate_logits, selected, lengths, w_out):
    prefix_rows = prefix_kv.reshape(NB * BLK, KV)
    blocks = prefix_rows.reshape(NB, BLK, KV).astype(F32)
    comp_keys = jnp.einsum(
        "bjd,j->bd", blocks[:, :, :DK], pooling[0], precision=lax.Precision.HIGHEST
    )
    comp_values = jnp.einsum(
        "bjd,j->bd", blocks[:, :, DK:], pooling[1], precision=lax.Precision.HIGHEST
    )
    comp = jnp.concatenate(
        [comp_keys, jnp.zeros((NB, 2 * LANES - DK), F32), comp_values], axis=-1
    ).astype(BF16)

    z = lax.axis_index("sib")
    c = lax.axis_index("ctx")
    ids = selected.reshape(-1)
    owner = ids // NB
    local = ids % NB
    plane = (owner // NC - z + NZ) % NZ
    offset = (owner % NC - c + NC) % NC
    place = offset * NZ + plane
    order = jnp.arange(ids.shape[0], dtype=jnp.int32)
    rank = jnp.sum(
        ((place[:, None] == place[None, :]) & (order[None, :] < order[:, None])).astype(jnp.int32),
        axis=1,
    )
    pos = ((plane * NC + offset) * CAP + rank).reshape(QB, TOPK)
    lanes = jnp.arange(LANES, dtype=jnp.int32)
    entry = jnp.where(lanes[None, :] < CAP, local[:, None] // 2, local[:, None] % 2)
    hit = (place[:, None, None] == jnp.arange(NC * NZ, dtype=jnp.int32)[None, :, None]) & (
        (rank[:, None] == lanes[None, :]) | (rank[:, None] + CAP == lanes[None, :])
    )[:, None, :]
    requests = jnp.sum(jnp.where(hit, entry[:, None, :], 0), axis=0).reshape(NC, NZ, LANES)

    gates = jax.nn.sigmoid(gate_logits.reshape(ROWS, 3 * HQ))
    head_flat = attend(
        pos,
        lengths,
        queries.reshape(ROWS, HQ * DK),
        suffix_kv.reshape(ROWS, KV).T,
        prefix_rows.T,
        comp,
        requests,
        gates,
    )
    summed = lax.psum_scatter(
        jnp.dot(head_flat, w_out, preferred_element_type=F32),
        "head",
        scatter_dimension=0,
        tiled=True,
    )
    return summed.astype(BF16).reshape(1, -1, DM)


def solution(mesh):
    return jax.shard_map(
        shards,
        mesh=mesh,
        in_specs=(
            P("sib", "ctx", "head", None),
            P("sib", "ctx", "head", None),
            P(("sib", "ctx"), "head", None),
            P(),
            P("sib", "ctx", "head", None),
            P("sib", "ctx", "head", None),
            P("sib"),
            P("head", None),
        ),
        out_specs=P("sib", ("ctx", "head"), None),
        check_vma=False,
    )
```

```python
import functools

import jax
import jax.numpy as jnp
from jax import lax
from jax.experimental import pallas as pl
from jax.experimental.pallas import tpu as pltpu
from jax.sharding import PartitionSpec as P

DK = 192
DV = 128
KV = DK + DV
HQ = 8
DM = 2560
BLK = 64
W = 512
ROWS = 512
NB = 32
TOPK = 16
QB = ROWS // BLK
NZ = 8
NC = 8
CAP = 3
PAIRS = NB // 2
CHUNK = 4
LANES = 128
TILE = HQ * BLK
NY = 4
OUT_ROWS = ROWS // NY
GROUP_ROWS = HQ * DV
HALF = GROUP_ROWS // 2
PIECE = HALF // 4
NTILE = 256
SCALE2 = DK ** (-0.5) * 1.4426950408889634
MESH = pl.DeviceIdType.MESH
BF16 = jnp.bfloat16
F32 = jnp.float32


def remote(source, target, send_sem, recv_sem, device):
    return pltpu.make_async_remote_copy(
        src_ref=source,
        dst_ref=target,
        send_sem=send_sem,
        recv_sem=recv_sem,
        device_id=device,
        device_id_type=MESH,
    )


def swap_halves(tile):
    return jnp.concatenate([tile[:, 64:], tile[:, :64]], axis=1)


def layer_kernel(
    len_ref,
    id_ref,
    pool_ref,
    gate_ref,
    q_ref,
    suffix_ref,
    prefix_ref,
    w_ref,
    out_ref,
    own,
    plus1,
    plus2,
    plus3,
    minus1,
    minus2,
    minus3,
    far,
    outgoing,
    incoming,
    comp_all,
    near,
    ask_table,
    asked,
    asked_smem,
    place_table,
    place_smem,
    q_raw,
    q_heads,
    gates_all,
    mixed,
    sel_kv,
    w_all,
    heads_out,
    heads_in,
    partial,
    load_sem,
    misc_sem,
    z_send,
    z_recv,
    x_send,
    x_recv,
    comp_send,
    comp_recv,
    ask_send,
    ask_recv,
    ask_load,
    halo_send,
    halo_recv,
    w_send,
    w_recv,
    twin_send,
    twin_recv,
    head_send,
    head_recv,
):
    z = lax.axis_index("sib")
    c = lax.axis_index("ctx")
    y = lax.axis_index("head")

    def z_peer(offset):
        return ((z + offset) % NZ, c, y)

    def c_peer(offset):
        return (z, (c + offset) % NC, y)

    def y_peer(offset):
        return (z, c, (y + offset) % NY)

    core = c % 2
    twin_device = (z, c + 1 - 2 * core, y)

    barrier = pltpu.get_barrier_semaphore()
    for offset in range(1, NZ):
        pl.semaphore_signal(barrier, inc=1, device_id=z_peer(offset), device_id_type=MESH)
    for offset in range(1, NC):
        pl.semaphore_signal(barrier, inc=1, device_id=c_peer(offset), device_id_type=MESH)
    for offset in range(1, NY):
        pl.semaphore_signal(barrier, inc=1, device_id=y_peer(offset), device_id_type=MESH)

    loads = [
        pltpu.make_async_copy(
            prefix_ref.at[:, pl.ds(pair * LANES, LANES)], own.at[pair], load_sem.at[pair]
        )
        for pair in range(PAIRS)
    ]
    for load in loads:
        load.start()
    q_load = pltpu.make_async_copy(q_ref, q_raw, misc_sem.at[0])
    q_load.start()
    near_load = pltpu.make_async_copy(suffix_ref, near.at[:, pl.ds(ROWS, ROWS)], misc_sem.at[1])
    near_load.start()
    w_load = pltpu.make_async_copy(w_ref, w_all.at[0], misc_sem.at[2])
    w_load.start()
    pl.semaphore_wait(barrier, NZ - 1 + NC - 1 + NY - 1)

    def comp_over_z(offset):
        return remote(
            comp_all.at[0, 0],
            comp_all.at[0, NZ - offset],
            comp_send.at[0, offset],
            comp_recv.at[0, NZ - offset],
            z_peer(offset),
        )

    def comp_over_c(offset):
        return remote(
            comp_all.at[0],
            comp_all.at[NC - offset],
            comp_send.at[1, offset],
            comp_recv.at[1, NC - offset],
            c_peer(offset),
        )

    def ask(offset):
        return remote(
            ask_table.at[offset],
            asked.at[NC - offset],
            ask_send.at[offset],
            ask_recv.at[NC - offset],
            c_peer(offset),
        )

    def halo():
        return remote(
            suffix_ref, near.at[:, pl.ds(0, ROWS)], halo_send.at[0], halo_recv.at[0], c_peer(1)
        )

    stages = {1: (own, plus1, plus2, plus3, far), -1: (own, minus1, minus2, minus3, far)}

    def z_chunks(way, step):
        if step < 3:
            return tuple(range(4))
        return (0, 1) if way == 1 else (2, 3)

    def z_copy(way, step, chunk):
        row = 0 if way == 1 else 1
        window = pl.ds(CHUNK * chunk, CHUNK)
        return remote(
            stages[way][step].at[window],
            stages[way][step + 1].at[window],
            z_send.at[row, step, chunk],
            z_recv.at[row, step, chunk],
            z_peer(way),
        )

    room = {0: 0, 1: 1, 7: 2, 2: 3, 6: 0, 3: 1, 5: 2, 4: 3}
    room_before = {6: 0, 3: 1, 5: 7, 4: 2}

    def w_copy(way, step, piece):
        row = 0 if way == 1 else 1
        rows = pl.ds(pl.multiple_of(core * HALF + piece * PIECE, PIECE), PIECE)
        near_slot = 3 if way == 1 else 1
        return remote(
            w_ref.at[rows] if step == 0 else w_all.at[near_slot, rows],
            w_all.at[near_slot if step == 0 else 2, rows],
            w_send.at[row, step, piece],
            w_recv.at[row, step, piece],
            y_peer(way),
        )

    def w_pieces(way, step):
        if step == 0:
            return (0, 1, 2, 3) if way == 1 else (2, 3, 0, 1)
        return (0, 1) if way == 1 else (2, 3)

    def twin_copy(slot, piece):
        rows = pl.ds(pl.multiple_of(core * HALF + piece * PIECE, PIECE), PIECE)
        return remote(
            w_all.at[slot, rows],
            w_all.at[slot, rows],
            twin_send.at[slot, piece],
            twin_recv.at[slot, piece],
            twin_device,
        )

    def twin_arrival(slot, piece):
        rows = pl.ds(pl.multiple_of((1 - core) * HALF + piece * PIECE, PIECE), PIECE)
        return remote(
            w_all.at[slot, rows],
            w_all.at[slot, rows],
            twin_send.at[slot, piece],
            twin_recv.at[slot, piece],
            twin_device,
        )

    def w_service(step, turn):
        for way in (1, -1):
            piece = w_pieces(way, step)[turn]
            w_copy(way, step, piece).wait_recv()
            if step == 0 and piece in w_pieces(way, 1):
                w_copy(way, 1, piece).start()
            if step == 0:
                twin_copy(3 if way == 1 else 1, piece).start()

    def w_far_twins(turn):
        for way in (1, -1):
            twin_copy(2, w_pieces(way, 1)[turn]).start()

    def head_copy(offset):
        return remote(
            heads_out.at[offset],
            heads_in.at[NY - offset],
            head_send.at[offset],
            head_recv.at[NY - offset],
            y_peer(offset),
        )

    def x_copy(plane, offset):
        return remote(
            outgoing.at[pl.ds((room[plane] * NC + offset) * CAP, CAP)],
            incoming.at[pl.ds((plane * NC + NC - offset) * CAP, CAP)],
            x_send.at[plane, offset],
            x_recv.at[plane, NC - offset],
            c_peer(offset),
        )

    left_half = lax.broadcasted_iota(jnp.int32, (KV // 2, LANES), 1) < BLK

    planes = {0: own, 7: plus1, 6: plus2, 5: plus3, 1: minus1, 2: minus2, 3: minus3, 4: far}

    def fill(plane):
        held = planes[plane]
        if plane in room_before:
            for offset in range(1, NC):
                x_copy(room_before[plane], offset).wait_send()

        def one(index, carry):
            offset = index // CAP
            slot = index % CAP
            pair = asked_smem[offset, plane, slot]
            half = asked_smem[offset, plane, CAP + slot]
            tile = held[pair]
            upper = tile[: KV // 2]
            lower = tile[KV // 2 :]
            first = half == 0
            kept_upper = jnp.where(first, upper, swap_halves(upper))
            kept_lower = jnp.where(first, swap_halves(lower), lower)
            outgoing[room[plane] * NC * CAP + index] = jnp.where(left_half, kept_upper, kept_lower)
            return carry

        lax.fori_loop(0, NC * CAP, one, 0)
        incoming[pl.ds(plane * NC * CAP, CAP)] = outgoing[pl.ds(room[plane] * NC * CAP, CAP)]

    def send_plane(plane):
        for offset in (2, 6, 4, 3, 5, 1, 7):
            x_copy(plane, offset).start()

    def forward(step, chunk):
        for way in (1, -1):
            if chunk in z_chunks(way, step):
                z_copy(way, step, chunk).wait_recv()
                if step < 3 and chunk in z_chunks(way, step + 1):
                    z_copy(way, step + 1, chunk).start()

    nt = (((1,), (1,)), ((), ()))

    halo().start()
    for way in (1, -1):
        w_copy(way, 0, w_pieces(way, 0)[0]).start()
    for load in loads:
        load.wait()
    for way in (1, -1):
        z_copy(way, 0, 0).start()

    ids = id_ref[...]
    owner = ids // NB
    local = ids % NB
    plane_of = (owner // NC - z + NZ) % NZ
    offset_of = (owner % NC - c + NC) % NC
    place = offset_of * NZ + plane_of
    square = (LANES, LANES)
    down = lax.broadcasted_iota(jnp.int32, square, 0)
    along = lax.broadcasted_iota(jnp.int32, square, 1)
    place_along = jnp.broadcast_to(place, square)
    place_down = jnp.sum(jnp.where(down == along, place_along, 0), axis=1, keepdims=True)
    rank = jnp.sum(
        jnp.where((place_down == place_along) & (down < along), 1, 0), axis=0, keepdims=True
    )
    landing = (plane_of * NC + offset_of) * CAP + jnp.minimum(rank, CAP - 1)
    place_table[...] = jnp.broadcast_to(landing, (8, LANES))
    wide = (NC * NZ, LANES)
    matches = lax.broadcasted_iota(jnp.int32, wide, 0) == place
    lane = lax.broadcasted_iota(jnp.int32, wide, 1)
    table = jnp.zeros(wide, jnp.int32)
    for slot in range(CAP):
        hit = matches & (rank == slot)
        pair_value = jnp.sum(jnp.where(hit, local // 2, 0), axis=1, keepdims=True)
        half_value = jnp.sum(jnp.where(hit, local % 2, 0), axis=1, keepdims=True)
        table = jnp.where(lane == slot, pair_value, table)
        table = jnp.where(lane == CAP + slot, half_value, table)
    ask_table[...] = table.reshape(NC, NZ, LANES)

    rows3 = 3 * NB
    down3 = lax.broadcasted_iota(jnp.int32, (rows3, LANES), 0)
    along3 = lax.broadcasted_iota(jnp.int32, (rows3, LANES), 1)

    def parts_of(row):
        weights = jnp.concatenate([pool_ref[row : row + 1, :]] * 2, axis=1)
        high = weights.astype(BF16).astype(F32)
        middle = (weights - high).astype(BF16).astype(F32)
        low = weights - high - middle
        return jnp.where(down3 < NB, high, jnp.where(down3 < 2 * NB, middle, low))

    key_parts = parts_of(0)
    value_parts = parts_of(1)

    def compress(pair, sums):
        mine = down3 % NB == 2 * pair + along3 // BLK
        tile = own[pair]
        keys = lax.dot_general(
            jnp.where(mine, key_parts, 0.0).astype(BF16),
            tile[:DK],
            nt,
            preferred_element_type=F32,
        )
        values = lax.dot_general(
            jnp.where(mine, value_parts, 0.0).astype(BF16),
            tile[DK:],
            nt,
            preferred_element_type=F32,
        )
        return sums[0] + keys, sums[1] + values

    key_sums, value_sums = lax.fori_loop(
        0, PAIRS, compress, (jnp.zeros((rows3, DK), F32), jnp.zeros((rows3, DV), F32))
    )
    comp_all[0, 0, :, :DK] = (
        key_sums[:NB] + key_sums[NB : 2 * NB] + key_sums[2 * NB :]
    ).astype(BF16)
    comp_all[0, 0, :, DK : 2 * LANES] = jnp.zeros((NB, 2 * LANES - DK), BF16)
    comp_all[0, 0, :, 2 * LANES :] = (
        value_sums[:NB] + value_sums[NB : 2 * NB] + value_sums[2 * NB :]
    ).astype(BF16)

    for offset in range(1, NC):
        ask(offset).start()
    ask_self = pltpu.make_async_copy(ask_table.at[0], asked_smem.at[0], ask_load.at[0])
    ask_self.start()
    place_copy = pltpu.make_async_copy(place_table, place_smem, misc_sem.at[3])
    place_copy.start()

    gates_all[...] = jax.nn.sigmoid(gate_ref[...]).T
    q_load.wait()
    for head in range(HQ):
        q_heads[head] = q_raw[:, head * DK : (head + 1) * DK]

    for offset in (4, 3, 5, 2, 6, 1, 7):
        comp_over_z(offset).start()
    for chunk in range(1, 4):
        for way in (1, -1):
            z_copy(way, 0, chunk).start()
    for turn in range(1, 4):
        for way in (1, -1):
            w_copy(way, 0, w_pieces(way, 0)[turn]).start()

    for offset in range(1, NC):
        ask(NC - offset).wait_recv()
        pltpu.make_async_copy(asked.at[offset], asked_smem.at[offset], ask_load.at[offset]).start()
    for offset in range(1, NC):
        pltpu.make_async_copy(asked.at[offset], asked_smem.at[offset], ask_load.at[offset]).wait()
    ask_self.wait()
    place_copy.wait()
    fill(0)
    for offset in range(1, NZ):
        comp_over_z(NZ - offset).wait_recv()
    for offset in (4, 2, 6, 3, 5, 1, 7):
        comp_over_c(offset).start()

    def queries_of(block):
        rows = pl.ds(pl.multiple_of(block * BLK, BLK), BLK)
        return q_heads[:, rows, :].reshape(TILE, DK)

    def gate_columns(block):
        rows = pl.ds(pl.multiple_of(block * BLK, BLK), BLK)
        return gates_all[rows, :]

    def softmax(scores, previous_max=None):
        top = jnp.max(scores, axis=-1, keepdims=True)
        if previous_max is not None:
            top = jnp.maximum(previous_max, top)
        weights = jnp.exp2(scores * SCALE2 - top * SCALE2)
        return top, weights, jnp.sum(weights, axis=-1, keepdims=True)

    near_load.wait()
    halo().wait_recv()

    def window_block(block, carry):
        start = pl.multiple_of((block // 2) * LANES, LANES)
        span = pl.ds(start, W + LANES)
        scores = jnp.dot(queries_of(block), near[:DK, span], preferred_element_type=F32)
        scores = scores.reshape(HQ, BLK, W + LANES)
        row = lax.broadcasted_iota(jnp.int32, (1, BLK, W + LANES), 1) + (block % 2) * BLK
        lane = lax.broadcasted_iota(jnp.int32, (1, BLK, W + LANES), 2)
        reach = jnp.where(c == 0, ROWS - start, 0)
        visible = (lane > row) & (lane <= row + W) & (lane >= reach)
        scores = jnp.where(visible, scores, -jnp.inf).reshape(TILE, W + LANES)
        _, weights, total = softmax(scores)
        result = lax.dot_general(
            weights.astype(BF16), near[DK:, span], nt, preferred_element_type=F32
        )
        result = result / total
        gates = gate_columns(block)
        for head in range(HQ):
            mixed[block, head * BLK : (head + 1) * BLK, :] = (
                result[head * BLK : (head + 1) * BLK]
                * gates[:, 2 * HQ + head : 2 * HQ + head + 1]
            )
        return carry

    window_block(0, 0)
    send_plane(0)

    def window_loop(block, carry):
        window_block(block, carry)

        @pl.when(block == 2)
        def _():
            forward(0, 0)

            w_service(0, 0)

        @pl.when(block == 4)
        def _():
            forward(0, 1)

        @pl.when(block == 6)
        def _():
            forward(0, 2)

        return carry

    lax.fori_loop(1, QB, window_loop, 0)

    for offset in range(1, NC):
        comp_over_c(NC - offset).wait_recv()

    half_keys = NZ * NC * NB // 2

    def comp_block(block, carry):
        queries = queries_of(block)
        comp_flat = comp_all.reshape(NZ * NC * NB, 3 * LANES)
        top = None
        for part in range(2):
            keys = pl.ds(part * half_keys, half_keys)
            scores = lax.dot_general(
                queries, comp_flat[keys, :DK], nt, preferred_element_type=F32
            )
            new_top, weights, total = softmax(scores, top)
            result = jnp.dot(
                weights.astype(BF16), comp_flat[keys, 2 * LANES :], preferred_element_type=F32
            )
            if part == 0:
                top, all_total, all_result = new_top, total, result
            else:
                decay = jnp.exp2((top - new_top) * SCALE2)
                all_total = all_total * decay + total
                all_result = all_result * decay + result
        result = all_result / all_total
        gates = gate_columns(block)
        for head in range(HQ):
            rows = slice(head * BLK, (head + 1) * BLK)
            mixed[block, rows, :] += result[rows] * gates[:, head : head + 1]
        return carry

    def comp_loop(block, carry):
        comp_block(block, carry)

        @pl.when(block == 0)
        def _():
            forward(0, 3)
            fill(1)
            fill(7)
            w_service(0, 1)

        @pl.when(block == 1)
        def _():
            send_plane(1)
            send_plane(7)
            forward(1, 0)

        @pl.when(block == 3)
        def _():
            forward(1, 1)
            w_service(0, 2)

        @pl.when(block == 5)
        def _():
            forward(1, 2)

        return carry

    lax.fori_loop(0, QB, comp_loop, 0)

    forward(1, 3)
    fill(2)
    fill(6)
    w_service(0, 3)
    forward(2, 0)
    send_plane(2)
    send_plane(6)
    forward(2, 1)
    w_service(1, 0)
    w_far_twins(0)
    forward(2, 2)
    forward(2, 3)
    fill(3)
    fill(5)
    forward(3, 0)
    send_plane(3)
    send_plane(5)
    forward(3, 2)
    w_service(1, 1)
    forward(3, 1)
    forward(3, 3)
    fill(4)
    w_load.wait()
    send_plane(4)
    w_far_twins(1)
    for plane in (0, 1, 7, 2, 6, 3, 5, 4):
        for offset in range(1, NC):
            x_copy(plane, NC - offset).wait_recv()

    def selected_block(turn, carry):
        target = NY - 1 - turn // 2
        block = 2 * ((y + target) % NY) + turn % 2
        for pair in range(TOPK // 2):
            first = incoming[place_smem[0, block * TOPK + 2 * pair]]
            second = incoming[place_smem[0, block * TOPK + 2 * pair + 1]]
            lanes = slice(pair * LANES, (pair + 1) * LANES)
            sel_kv[: KV // 2, lanes] = jnp.where(left_half, first, swap_halves(second))
            sel_kv[KV // 2 :, lanes] = jnp.where(left_half, swap_halves(first), second)
        for peer in range(1, NY):

            @pl.when(turn == 2 * (NY - peer))
            def _():
                head_copy(peer).start()

        scores = jnp.dot(queries_of(block), sel_kv[:DK, :], preferred_element_type=F32)
        _, weights, total = softmax(scores)
        result = lax.dot_general(
            weights.astype(BF16), sel_kv[DK:, :], nt, preferred_element_type=F32
        )
        result = result / total
        gates = gate_columns(block)
        first_row = pl.multiple_of((turn % 2) * BLK, BLK)
        inside = (
            lax.broadcasted_iota(jnp.int32, (BLK, DV), 0) + c * ROWS + block * BLK < len_ref[0]
        )
        for head in range(HQ):
            rows = slice(head * BLK, (head + 1) * BLK)
            value = (
                mixed[block, rows, :] + result[rows] * gates[:, HQ + head : HQ + head + 1]
            )
            heads_out[target, pl.ds(first_row, BLK), head * DV : (head + 1) * DV] = jnp.where(
                inside, value, 0.0
            ).astype(BF16)
        return carry

    lax.fori_loop(0, QB, selected_block, 0)

    for slot in range(1, NY):
        for piece in range(4):
            twin_arrival(slot, piece).wait_recv()
    for peer in (3, 2):
        head_copy(peer).wait_recv()

    def project_near(index, carry):
        columns = pl.ds(pl.multiple_of(index * NTILE, NTILE), NTILE)
        total = jnp.dot(heads_out[0], w_all[0, :, columns], preferred_element_type=F32)
        total += jnp.dot(heads_in[1], w_all[1, :, columns], preferred_element_type=F32)
        total += jnp.dot(heads_in[2], w_all[2, :, columns], preferred_element_type=F32)
        partial[:, columns] = total
        return carry

    lax.fori_loop(0, DM // NTILE, project_near, 0)
    head_copy(1).wait_recv()

    def project_last(index, carry):
        columns = pl.ds(pl.multiple_of(index * NTILE, NTILE), NTILE)
        total = jnp.dot(heads_in[3], w_all[3, :, columns], preferred_element_type=F32)
        out_ref[:, columns] = (partial[:, columns] + total).astype(BF16)
        return carry

    lax.fori_loop(0, DM // NTILE, project_last, 0)

    for offset in range(1, NZ):
        comp_over_z(offset).wait_send()
    for offset in range(1, NC):
        comp_over_c(offset).wait_send()
        ask(offset).wait_send()
        for plane in (6, 3, 5, 4):
            x_copy(plane, offset).wait_send()
    halo().wait_send()
    for way in (1, -1):
        for step in range(2):
            for piece in w_pieces(way, step):
                w_copy(way, step, piece).wait_send()
    for slot in range(1, NY):
        head_copy(slot).wait_send()
        for piece in range(4):
            twin_copy(slot, piece).wait_send()
    for step in range(4):
        for way in (1, -1):
            for chunk in z_chunks(way, step):
                z_copy(way, step, chunk).wait_send()


def shards(queries, suffix_kv, prefix_kv, pooling, gate_logits, selected, lengths, w_out):
    anywhere = pl.BlockSpec(memory_space=pl.ANY)
    vmem = pl.BlockSpec(memory_space=pltpu.VMEM)
    smem = pl.BlockSpec(memory_space=pltpu.SMEM)
    plane = pltpu.VMEM((PAIRS, KV, LANES), BF16)
    dma = pltpu.SemaphoreType.DMA
    out = pl.pallas_call(
        layer_kernel,
        name="layer",
        out_shape=jax.ShapeDtypeStruct((OUT_ROWS, DM), BF16),
        in_specs=[smem, vmem, vmem, vmem, anywhere, anywhere, anywhere, anywhere],
        out_specs=vmem,
        scratch_shapes=[plane] * 8
        + [
            pltpu.VMEM((4 * NC * CAP, KV // 2, LANES), BF16),
            pltpu.VMEM((NZ * NC * CAP, KV // 2, LANES), BF16),
            pltpu.VMEM((NC, NZ, NB, 3 * LANES), BF16),
            pltpu.VMEM((KV, 2 * ROWS), BF16),
            pltpu.VMEM((NC, NZ, LANES), jnp.int32),
            pltpu.VMEM((NC, NZ, LANES), jnp.int32),
            pltpu.SMEM((NC, NZ, LANES), jnp.int32),
            pltpu.VMEM((8, LANES), jnp.int32),
            pltpu.SMEM((8, LANES), jnp.int32),
            pltpu.VMEM((ROWS, HQ * DK), BF16),
            pltpu.VMEM((HQ, ROWS, DK), BF16),
            pltpu.VMEM((ROWS, 3 * HQ), F32),
            pltpu.VMEM((QB, TILE, DV), F32),
            pltpu.VMEM((KV, TOPK * BLK), BF16),
            pltpu.VMEM((NY, GROUP_ROWS, DM), BF16),
            pltpu.VMEM((NY, OUT_ROWS, GROUP_ROWS), BF16),
            pltpu.VMEM((NY, OUT_ROWS, GROUP_ROWS), BF16),
            pltpu.VMEM((OUT_ROWS, DM), F32),
            dma((PAIRS,)),
            dma((4,)),
            dma((2, 4, 4)),
            dma((2, 4, 4)),
            dma((NZ, NC)),
            dma((NZ, NC)),
            dma((2, NC)),
            dma((2, NC)),
            dma((NC,)),
            dma((NC,)),
            dma((NC,)),
            dma((1,)),
            dma((1,)),
            dma((2, 2, 4)),
            dma((2, 2, 4)),
            dma((NY, 4)),
            dma((NY, 4)),
            dma((NY,)),
            dma((NY,)),
        ],
        compiler_params=pltpu.CompilerParams(
            collective_id=0, has_side_effects=True, vmem_limit_bytes=67_043_328
        ),
    )(
        lengths,
        selected.reshape(1, QB * TOPK),
        pooling,
        gate_logits.reshape(ROWS, 3 * HQ).T,
        queries.reshape(ROWS, HQ * DK),
        suffix_kv.reshape(ROWS, KV).T,
        prefix_kv.reshape(NB * BLK, KV).T,
        w_out,
    )
    return out.reshape(1, OUT_ROWS, DM)


def solution(mesh):
    return jax.shard_map(
        shards,
        mesh=mesh,
        in_specs=(
            P("sib", "ctx", "head", None),
            P("sib", "ctx", "head", None),
            P(("sib", "ctx"), "head", None),
            P(),
            P("sib", "ctx", "head", None),
            P("sib", "ctx", "head", None),
            P("sib"),
            P("head", None),
        ),
        out_specs=P("sib", ("ctx", "head"), None),
        check_vma=False,
    )
```

```python
import functools

import jax
import jax.numpy as jnp
from jax import lax
from jax.experimental import pallas as pl
from jax.experimental.pallas import tpu as pltpu
from jax.sharding import PartitionSpec as P

DK = 192
DV = 128
KV = DK + DV
HQ = 8
DM = 2560
BLK = 64
W = 512
ROWS = 512
NB = 32
TOPK = 16
QB = ROWS // BLK
NZ = 8
NC = 8
CAP = 3
PAIRS = NB // 2
CHUNK = 4
LANES = 128
TILE = HQ * BLK
NY = 4
NX = 4
OUT_ROWS = ROWS // NY
GROUP_ROWS = HQ * DV
HALF = GROUP_ROWS // 2
PIECE = HALF // 4
NTILE = 256
SCALE2 = DK ** (-0.5) * 1.4426950408889634
MESH = pl.DeviceIdType.MESH
BF16 = jnp.bfloat16
F32 = jnp.float32


def remote(source, target, send_sem, recv_sem, device):
    return pltpu.make_async_remote_copy(
        src_ref=source,
        dst_ref=target,
        send_sem=send_sem,
        recv_sem=recv_sem,
        device_id=device,
        device_id_type=MESH,
    )


def swap_halves(tile):
    return jnp.concatenate([tile[:, 64:], tile[:, :64]], axis=1)


def layer_kernel(
    len_ref,
    id_ref,
    pool_ref,
    gate_ref,
    q_ref,
    suffix_ref,
    prefix_ref,
    w_ref,
    out_ref,
    own,
    plus1,
    plus2,
    plus3,
    minus1,
    minus2,
    minus3,
    far,
    outgoing,
    incoming,
    comp_all,
    near,
    ask_table,
    asked,
    asked_smem,
    place_table,
    place_smem,
    q_raw,
    q_heads,
    gates_all,
    mixed,
    sel_kv,
    w_all,
    heads_out,
    heads_in,
    partial,
    load_sem,
    misc_sem,
    z_send,
    z_recv,
    x_send,
    x_recv,
    comp_send,
    comp_recv,
    ask_send,
    ask_recv,
    ask_load,
    halo_send,
    halo_recv,
    w_send,
    w_recv,
    twin_send,
    twin_recv,
    head_send,
    head_recv,
):
    z = lax.axis_index("sib")
    c = lax.axis_index("ctx")
    y = lax.axis_index("head")

    def z_peer(offset):
        return ((z + offset) % NZ, c, y)

    def c_peer(offset):
        return (z, (c + offset) % NC, y)

    def y_peer(offset):
        return (z, c, (y + offset) % NY)

    core = c % 2
    twin_device = (z, c + 1 - 2 * core, y)

    barrier = pltpu.get_barrier_semaphore()
    for offset in range(1, NZ):
        pl.semaphore_signal(barrier, inc=1, device_id=z_peer(offset), device_id_type=MESH)
    for offset in range(1, NC):
        pl.semaphore_signal(barrier, inc=1, device_id=c_peer(offset), device_id_type=MESH)
    for offset in range(1, NY):
        pl.semaphore_signal(barrier, inc=1, device_id=y_peer(offset), device_id_type=MESH)

    loads = [
        pltpu.make_async_copy(
            prefix_ref.at[:, pl.ds(pair * LANES, LANES)], own.at[pair], load_sem.at[pair]
        )
        for pair in range(PAIRS)
    ]
    for load in loads:
        load.start()
    q_load = pltpu.make_async_copy(q_ref, q_raw, misc_sem.at[0])
    q_load.start()
    near_load = pltpu.make_async_copy(suffix_ref, near.at[:, pl.ds(ROWS, ROWS)], misc_sem.at[1])
    near_load.start()
    w_load = pltpu.make_async_copy(w_ref, w_all.at[0], misc_sem.at[2])
    w_load.start()
    pl.semaphore_wait(barrier, NZ - 1 + NC - 1 + NY - 1)

    def comp_over_z(offset):
        return remote(
            comp_all.at[0, 0],
            comp_all.at[0, NZ - offset],
            comp_send.at[0, offset],
            comp_recv.at[0, NZ - offset],
            z_peer(offset),
        )

    def comp_over_c(chips):
        return remote(
            comp_all.at[0],
            comp_all.at[NX - chips],
            comp_send.at[1, chips],
            comp_recv.at[1, NX - chips],
            c_peer(2 * chips),
        )

    def comp_to_twin(slot):
        return remote(
            comp_all.at[slot],
            comp_all.at[NX + slot],
            comp_send.at[1, NX + slot],
            comp_recv.at[1, NX + slot],
            twin_device,
        )

    def ask(offset):
        return remote(
            ask_table.at[pl.ds(offset, 1)],
            asked.at[pl.ds(NC - offset, 1)],
            ask_send.at[offset],
            ask_recv.at[NC - offset],
            c_peer(offset),
        )

    def halo():
        return remote(
            suffix_ref, near.at[:, pl.ds(0, ROWS)], halo_send.at[0], halo_recv.at[0], c_peer(1)
        )

    stages = {1: (own, plus1, plus2, plus3, far), -1: (own, minus1, minus2, minus3, far)}

    def z_chunks(way, step):
        if step < 3:
            return tuple(range(4))
        return (0, 1) if way == 1 else (2, 3)

    def z_copy(way, step, chunk):
        row = 0 if way == 1 else 1
        window = pl.ds(CHUNK * chunk, CHUNK)
        return remote(
            stages[way][step].at[window],
            stages[way][step + 1].at[window],
            z_send.at[row, step, chunk],
            z_recv.at[row, step, chunk],
            z_peer(way),
        )

    room = {0: 0, 1: 1, 7: 2, 2: 3, 6: 0, 3: 1, 5: 2, 4: 3}
    room_before = {6: 0, 3: 1, 5: 7, 4: 2}

    def w_copy(way, step, piece):
        row = 0 if way == 1 else 1
        rows = pl.ds(pl.multiple_of(core * HALF + piece * PIECE, PIECE), PIECE)
        near_slot = 3 if way == 1 else 1
        return remote(
            w_ref.at[rows] if step == 0 else w_all.at[near_slot, rows],
            w_all.at[near_slot if step == 0 else 2, rows],
            w_send.at[row, step, piece],
            w_recv.at[row, step, piece],
            y_peer(way),
        )

    def w_pieces(way, step):
        if step == 0:
            return (0, 1, 2, 3) if way == 1 else (2, 3, 0, 1)
        return (0, 1) if way == 1 else (2, 3)

    def twin_copy(slot, piece):
        rows = pl.ds(pl.multiple_of(core * HALF + piece * PIECE, PIECE), PIECE)
        return remote(
            w_all.at[slot, rows],
            w_all.at[slot, rows],
            twin_send.at[slot, piece],
            twin_recv.at[slot, piece],
            twin_device,
        )

    def twin_arrival(slot, piece):
        rows = pl.ds(pl.multiple_of((1 - core) * HALF + piece * PIECE, PIECE), PIECE)
        return remote(
            w_all.at[slot, rows],
            w_all.at[slot, rows],
            twin_send.at[slot, piece],
            twin_recv.at[slot, piece],
            twin_device,
        )

    def w_service(step, turn):
        for way in (1, -1):
            piece = w_pieces(way, step)[turn]
            w_copy(way, step, piece).wait_recv()
            if step == 0 and piece in w_pieces(way, 1):
                w_copy(way, 1, piece).start()
            if step == 0:
                twin_copy(3 if way == 1 else 1, piece).start()

    def w_far_twins(turn):
        for way in (1, -1):
            twin_copy(2, w_pieces(way, 1)[turn]).start()

    def head_copy(offset, part):
        rows = pl.ds(part * BLK, BLK)
        return remote(
            heads_out.at[offset, rows],
            heads_in.at[NY - offset, rows],
            head_send.at[offset, part],
            head_recv.at[NY - offset, part],
            y_peer(offset),
        )

    def x_copy(plane, offset):
        return remote(
            outgoing.at[pl.ds((room[plane] * NC + offset) * CAP, CAP)],
            incoming.at[pl.ds((plane * NC + NC - offset) * CAP, CAP)],
            x_send.at[plane, offset],
            x_recv.at[plane, NC - offset],
            c_peer(offset),
        )

    left_half = lax.broadcasted_iota(jnp.int32, (KV // 2, LANES), 1) < BLK

    planes = {0: own, 7: plus1, 6: plus2, 5: plus3, 1: minus1, 2: minus2, 3: minus3, 4: far}

    def exchange(plane):
        held = planes[plane]
        if plane in room_before:
            for offset in range(1, NC):
                x_copy(room_before[plane], offset).wait_send()

        def peer_at(turn):
            offset = turn * 0
            for index, value in enumerate((4, 5, 3, 2, 6, 7, 1)):
                offset = jnp.where(turn == index, value, offset)
            return offset

        def serve(turn, carry):
            offset = peer_at(turn)
            for slot in range(CAP):
                pair = asked_smem[offset, plane * 8 + slot]
                half = asked_smem[offset, plane * 8 + CAP + slot]
                tile = held[pair]
                upper = tile[: KV // 2]
                lower = tile[KV // 2 :]
                first = half == 0
                kept_upper = jnp.where(first, upper, swap_halves(upper))
                kept_lower = jnp.where(first, swap_halves(lower), lower)
                outgoing[(room[plane] * NC + offset) * CAP + slot] = jnp.where(
                    left_half, kept_upper, kept_lower
                )

            @pl.when(turn >= 1)
            def _():
                x_copy(plane, peer_at(turn - 1)).start()

            return carry

        lax.fori_loop(0, NC, serve, 0)
        incoming[pl.ds(plane * NC * CAP, CAP)] = outgoing[pl.ds(room[plane] * NC * CAP, CAP)]

    def forward(step, chunk):
        for way in (1, -1):
            if chunk in z_chunks(way, step):
                z_copy(way, step, chunk).wait_recv()
                if step < 3 and chunk in z_chunks(way, step + 1):
                    z_copy(way, step + 1, chunk).start()

    nt = (((1,), (1,)), ((), ()))

    halo().start()
    for way in (1, -1):
        w_copy(way, 0, w_pieces(way, 0)[0]).start()
    for load in loads:
        load.wait()
    for chunk in range(3):
        for way in (1, -1):
            z_copy(way, 0, chunk).start()

    ids = jnp.concatenate([id_ref[0, block] for block in range(QB)], axis=1)
    owner = ids // NB
    local = ids % NB
    plane_of = (owner // NC - z + NZ) % NZ
    offset_of = (owner % NC - c + NC) % NC
    place = offset_of * NZ + plane_of
    square = (LANES, LANES)
    down = lax.broadcasted_iota(jnp.int32, square, 0)
    along = lax.broadcasted_iota(jnp.int32, square, 1)
    place_along = jnp.broadcast_to(place, square)
    place_down = jnp.sum(jnp.where(down == along, place_along, 0), axis=1, keepdims=True)
    rank = jnp.sum(
        jnp.where((place_down == place_along) & (down < along), 1, 0), axis=0, keepdims=True
    )
    landing = (plane_of * NC + offset_of) * CAP + jnp.minimum(rank, CAP - 1)
    place_table[...] = jnp.broadcast_to(landing, (8, LANES))
    wide = (NC * NZ, LANES)
    matches = lax.broadcasted_iota(jnp.int32, wide, 0) == place
    lane = lax.broadcasted_iota(jnp.int32, wide, 1)
    table = jnp.zeros(wide, jnp.int32)
    own_lanes = lane // 8 == lax.broadcasted_iota(jnp.int32, wide, 0) % NZ
    for slot in range(CAP):
        hit = matches & (rank == slot)
        pair_value = jnp.sum(jnp.where(hit, local // 2, 0), axis=1, keepdims=True)
        half_value = jnp.sum(jnp.where(hit, local % 2, 0), axis=1, keepdims=True)
        table = jnp.where(own_lanes & (lane % 8 == slot), pair_value, table)
        table = jnp.where(own_lanes & (lane % 8 == CAP + slot), half_value, table)
    ask_table[...] = jnp.sum(table.reshape(NC, NZ, LANES), axis=1)

    rows3 = 3 * NB
    down3 = lax.broadcasted_iota(jnp.int32, (rows3, LANES), 0)
    along3 = lax.broadcasted_iota(jnp.int32, (rows3, LANES), 1)

    def parts_of(row):
        weights = jnp.concatenate([pool_ref[row : row + 1, :]] * 2, axis=1)
        high = weights.astype(BF16).astype(F32)
        middle = (weights - high).astype(BF16).astype(F32)
        low = weights - high - middle
        return jnp.where(down3 < NB, high, jnp.where(down3 < 2 * NB, middle, low))

    key_parts = parts_of(0)
    value_parts = parts_of(1)

    def compress(pair, sums):
        mine = down3 % NB == 2 * pair + along3 // BLK
        tile = own[pair]
        keys = lax.dot_general(
            jnp.where(mine, key_parts, 0.0).astype(BF16),
            tile[:DK],
            nt,
            preferred_element_type=F32,
        )
        values = lax.dot_general(
            jnp.where(mine, value_parts, 0.0).astype(BF16),
            tile[DK:],
            nt,
            preferred_element_type=F32,
        )
        return sums[0] + keys, sums[1] + values

    key_sums, value_sums = lax.fori_loop(
        0, PAIRS, compress, (jnp.zeros((rows3, DK), F32), jnp.zeros((rows3, DV), F32))
    )
    comp_all[0, 0, :, :DK] = (
        key_sums[:NB] + key_sums[NB : 2 * NB] + key_sums[2 * NB :]
    ).astype(BF16)
    comp_all[0, 0, :, DK : 2 * LANES] = jnp.zeros((NB, 2 * LANES - DK), BF16)
    comp_all[0, 0, :, 2 * LANES :] = (
        value_sums[:NB] + value_sums[NB : 2 * NB] + value_sums[2 * NB :]
    ).astype(BF16)

    for offset in range(1, NC):
        ask(offset).start()
    ask_self = pltpu.make_async_copy(
        ask_table.at[pl.ds(0, 1)], asked.at[pl.ds(0, 1)], ask_load.at[0]
    )
    ask_self.start()
    place_copy = pltpu.make_async_copy(place_table, place_smem, misc_sem.at[3])
    place_copy.start()
    gates_all[...] = jax.nn.sigmoid(gate_ref[...]).T
    for offset in (4, 3, 5, 2, 6, 1, 7):
        comp_over_z(offset).start()
    for way in (1, -1):
        z_copy(way, 0, 3).start()
    for turn in range(1, 4):
        for way in (1, -1):
            w_copy(way, 0, w_pieces(way, 0)[turn]).start()

    q_load.wait()
    for head in range(HQ):
        q_heads[head] = q_raw[:, head * DK : (head + 1) * DK]

    for offset in range(1, NC):
        ask(NC - offset).wait_recv()
    ask_self.wait()
    ask_all = pltpu.make_async_copy(asked, asked_smem, ask_load.at[1])
    ask_all.start()
    ask_all.wait()
    place_copy.wait()
    exchange(0)

    def queries_of(block):
        rows = pl.ds(pl.multiple_of(block * BLK, BLK), BLK)
        return q_heads[:, rows, :].reshape(TILE, DK)

    def gate_columns(block):
        rows = pl.ds(pl.multiple_of(block * BLK, BLK), BLK)
        return gates_all[rows, :]

    def softmax(scores, previous_max=None):
        top = jnp.max(scores, axis=-1, keepdims=True)
        if previous_max is not None:
            top = jnp.maximum(previous_max, top)
        weights = jnp.exp2(scores * SCALE2 - top * SCALE2)
        return top, weights, jnp.sum(weights, axis=-1, keepdims=True)

    near_load.wait()
    halo().wait_recv()

    def window_block(block, carry):
        start = pl.multiple_of((block // 2) * LANES, LANES)
        span = pl.ds(start, W + LANES)
        scores = jnp.dot(queries_of(block), near[:DK, span], preferred_element_type=F32)
        scores = scores.reshape(HQ, BLK, W + LANES)
        row = lax.broadcasted_iota(jnp.int32, (1, BLK, W + LANES), 1) + (block % 2) * BLK
        lane = lax.broadcasted_iota(jnp.int32, (1, BLK, W + LANES), 2)
        reach = jnp.where(c == 0, ROWS - start, 0)
        visible = (lane > row) & (lane <= row + W) & (lane >= reach)
        scores = jnp.where(visible, scores, -jnp.inf).reshape(TILE, W + LANES)
        _, weights, total = softmax(scores)
        result = lax.dot_general(
            weights.astype(BF16), near[DK:, span], nt, preferred_element_type=F32
        )
        result = result / total
        gates = gate_columns(block)
        for head in range(HQ):
            mixed[block, head * BLK : (head + 1) * BLK, :] = (
                result[head * BLK : (head + 1) * BLK]
                * gates[:, 2 * HQ + head : 2 * HQ + head + 1]
            )
        return carry

    def window_loop(block, carry):
        window_block(block, carry)

        @pl.when(block == 2)
        def _():
            forward(0, 0)

        @pl.when(block == 5)
        def _():
            forward(0, 1)

        return carry

    lax.fori_loop(0, QB, window_loop, 0)

    for offset in range(1, NZ):
        comp_over_z(NZ - offset).wait_recv()
    for chips in (2, 1, 3):
        comp_over_c(chips).start()
    comp_to_twin(0).start()
    forward(0, 2)
    w_service(0, 0)
    forward(0, 3)
    exchange(1)
    exchange(7)
    for chips in (1, 3, 2):
        comp_over_c(NX - chips).wait_recv()
        comp_to_twin(chips).start()
    w_service(0, 1)
    for slot in range(NX):
        comp_to_twin(slot).wait_recv()

    half_keys = NZ * NC * NB // 2

    def comp_block(block, carry):
        queries = queries_of(block)
        comp_flat = comp_all.reshape(NZ * NC * NB, 3 * LANES)
        top = None
        for part in range(2):
            keys = pl.ds(part * half_keys, half_keys)
            scores = lax.dot_general(
                queries, comp_flat[keys, :DK], nt, preferred_element_type=F32
            )
            new_top, weights, total = softmax(scores, top)
            result = jnp.dot(
                weights.astype(BF16), comp_flat[keys, 2 * LANES :], preferred_element_type=F32
            )
            if part == 0:
                top, all_total, all_result = new_top, total, result
            else:
                decay = jnp.exp2((top - new_top) * SCALE2)
                all_total = all_total * decay + total
                all_result = all_result * decay + result
        result = all_result / all_total
        gates = gate_columns(block)
        for head in range(HQ):
            rows = slice(head * BLK, (head + 1) * BLK)
            mixed[block, rows, :] += result[rows] * gates[:, head : head + 1]
        return carry

    def comp_loop(block, carry):
        comp_block(block, carry)

        @pl.when(block == 0)
        def _():
            forward(1, 0)

        @pl.when(block == 2)
        def _():
            forward(1, 1)

        @pl.when(block == 4)
        def _():
            forward(1, 2)
            w_service(0, 2)

        @pl.when(block == 6)
        def _():
            forward(1, 3)
            exchange(2)
            exchange(6)

        return carry

    lax.fori_loop(0, QB, comp_loop, 0)

    w_service(0, 3)
    forward(2, 0)
    forward(2, 1)
    w_service(1, 0)
    w_far_twins(0)
    forward(2, 2)
    forward(2, 3)
    exchange(3)
    exchange(5)
    forward(3, 0)
    forward(3, 2)
    w_service(1, 1)
    forward(3, 1)
    forward(3, 3)
    exchange(4)
    w_load.wait()
    w_far_twins(1)
    for plane in (0, 1, 7, 2, 6, 3, 5, 4):
        for offset in range(1, NC):
            x_copy(plane, NC - offset).wait_recv()

    def selected_block(turn, carry):
        group = turn // 2
        target = jnp.where(group == 0, 2, jnp.where(group == 1, 3, jnp.where(group == 2, 1, 0)))
        block = 2 * ((y + target) % NY) + turn % 2
        for pair in range(TOPK // 2):
            first = incoming[place_smem[0, block * TOPK + 2 * pair]]
            second = incoming[place_smem[0, block * TOPK + 2 * pair + 1]]
            lanes = slice(pair * LANES, (pair + 1) * LANES)
            sel_kv[: KV // 2, lanes] = jnp.where(left_half, first, swap_halves(second))
            sel_kv[KV // 2 :, lanes] = jnp.where(left_half, swap_halves(first), second)
        for done in range(QB - 2):

            @pl.when(turn == done + 1)
            def _():
                head_copy((2, 3, 1)[done // 2], done % 2).start()

        scores = jnp.dot(queries_of(block), sel_kv[:DK, :], preferred_element_type=F32)
        _, weights, total = softmax(scores)
        result = lax.dot_general(
            weights.astype(BF16), sel_kv[DK:, :], nt, preferred_element_type=F32
        )
        result = result / total
        gates = gate_columns(block)
        first_row = pl.multiple_of((turn % 2) * BLK, BLK)
        inside = (
            lax.broadcasted_iota(jnp.int32, (BLK, DV), 0) + c * ROWS + block * BLK < len_ref[0]
        )
        for head in range(HQ):
            rows = slice(head * BLK, (head + 1) * BLK)
            value = (
                mixed[block, rows, :] + result[rows] * gates[:, HQ + head : HQ + head + 1]
            )
            heads_out[target, pl.ds(first_row, BLK), head * DV : (head + 1) * DV] = jnp.where(
                inside, value, 0.0
            ).astype(BF16)
        return carry

    lax.fori_loop(0, QB, selected_block, 0)

    for slot in range(1, NY):
        for piece in range(4):
            twin_arrival(slot, piece).wait_recv()
    for part in range(2):
        head_copy(2, part).wait_recv()

    def project_near(index, carry):
        columns = pl.ds(pl.multiple_of(index * NTILE, NTILE), NTILE)
        total = jnp.dot(heads_out[0], w_all[0, :, columns], preferred_element_type=F32)
        total += jnp.dot(heads_in[2], w_all[2, :, columns], preferred_element_type=F32)
        partial[:, columns] = total
        return carry

    lax.fori_loop(0, DM // NTILE, project_near, 0)
    for peer in (3, 1):
        for part in range(2):
            head_copy(peer, part).wait_recv()

    def project_last(index, carry):
        columns = pl.ds(pl.multiple_of(index * NTILE, NTILE), NTILE)
        total = jnp.dot(heads_in[1], w_all[1, :, columns], preferred_element_type=F32)
        total += jnp.dot(heads_in[3], w_all[3, :, columns], preferred_element_type=F32)
        out_ref[:, columns] = (partial[:, columns] + total).astype(BF16)
        return carry

    lax.fori_loop(0, DM // NTILE, project_last, 0)

    for offset in range(1, NZ):
        comp_over_z(offset).wait_send()
    for offset in range(1, NC):
        ask(offset).wait_send()
        for plane in (6, 3, 5, 4):
            x_copy(plane, offset).wait_send()
    halo().wait_send()
    for chips in range(1, NX):
        comp_over_c(chips).wait_send()
    for slot in range(NX):
        comp_to_twin(slot).wait_send()
    for way in (1, -1):
        for step in range(2):
            for piece in w_pieces(way, step):
                w_copy(way, step, piece).wait_send()
    for slot in range(1, NY):
        for part in range(2):
            head_copy(slot, part).wait_send()
        for piece in range(4):
            twin_copy(slot, piece).wait_send()
    for step in range(4):
        for way in (1, -1):
            for chunk in z_chunks(way, step):
                z_copy(way, step, chunk).wait_send()


def shards(queries, suffix_kv, prefix_kv, pooling, gate_logits, selected, lengths, w_out):
    anywhere = pl.BlockSpec(memory_space=pl.ANY)
    vmem = pl.BlockSpec(memory_space=pltpu.VMEM)
    smem = pl.BlockSpec(memory_space=pltpu.SMEM)
    plane = pltpu.VMEM((PAIRS, KV, LANES), BF16)
    dma = pltpu.SemaphoreType.DMA
    out = pl.pallas_call(
        layer_kernel,
        name="layer",
        out_shape=jax.ShapeDtypeStruct((OUT_ROWS, DM), BF16),
        in_specs=[smem, vmem, vmem, vmem, anywhere, anywhere, anywhere, anywhere],
        out_specs=vmem,
        scratch_shapes=[plane] * 8
        + [
            pltpu.VMEM((4 * NC * CAP, KV // 2, LANES), BF16),
            pltpu.VMEM((NZ * NC * CAP, KV // 2, LANES), BF16),
            pltpu.VMEM((NC, NZ, NB, 3 * LANES), BF16),
            pltpu.VMEM((KV, 2 * ROWS), BF16),
            pltpu.VMEM((NC, LANES), jnp.int32),
            pltpu.VMEM((NC, LANES), jnp.int32),
            pltpu.SMEM((NC, LANES), jnp.int32),
            pltpu.VMEM((8, LANES), jnp.int32),
            pltpu.SMEM((8, LANES), jnp.int32),
            pltpu.VMEM((ROWS, HQ * DK), BF16),
            pltpu.VMEM((HQ, ROWS, DK), BF16),
            pltpu.VMEM((ROWS, 3 * HQ), F32),
            pltpu.VMEM((QB, TILE, DV), F32),
            pltpu.VMEM((KV, TOPK * BLK), BF16),
            pltpu.VMEM((NY, GROUP_ROWS, DM), BF16),
            pltpu.VMEM((NY, OUT_ROWS, GROUP_ROWS), BF16),
            pltpu.VMEM((NY, OUT_ROWS, GROUP_ROWS), BF16),
            pltpu.VMEM((OUT_ROWS, DM), F32),
            dma((PAIRS,)),
            dma((4,)),
            dma((2, 4, 4)),
            dma((2, 4, 4)),
            dma((NZ, NC)),
            dma((NZ, NC)),
            dma((2, NC)),
            dma((2, NC)),
            dma((NC,)),
            dma((NC,)),
            dma((2,)),
            dma((1,)),
            dma((1,)),
            dma((2, 2, 4)),
            dma((2, 2, 4)),
            dma((NY, 4)),
            dma((NY, 4)),
            dma((NY, 2)),
            dma((NY, 2)),
        ],
        compiler_params=pltpu.CompilerParams(
            collective_id=0, has_side_effects=True, vmem_limit_bytes=67_043_328
        ),
    )(
        lengths,
        selected,
        pooling,
        gate_logits.reshape(ROWS, 3 * HQ).T,
        queries.reshape(ROWS, HQ * DK),
        suffix_kv.reshape(ROWS, KV).T,
        prefix_kv.reshape(NB * BLK, KV).T,
        w_out,
    )
    return out.reshape(1, OUT_ROWS, DM)


def solution(mesh):
    return jax.shard_map(
        shards,
        mesh=mesh,
        in_specs=(
            P("sib", "ctx", "head", None),
            P("sib", "ctx", "head", None),
            P(("sib", "ctx"), "head", None),
            P(),
            P("sib", "ctx", "head", None),
            P("sib", "ctx", "head", None),
            P("sib"),
            P("head", None),
        ),
        out_specs=P("sib", ("ctx", "head"), None),
        check_vma=False,
    )
```

```python
import functools

import jax
import jax.numpy as jnp
from jax import lax
from jax.experimental import pallas as pl
from jax.experimental.pallas import tpu as pltpu
from jax.sharding import PartitionSpec as P

DK = 192
DV = 128
KV = DK + DV
HQ = 8
DM = 2560
BLK = 64
W = 512
ROWS = 512
NB = 32
TOPK = 16
QB = ROWS // BLK
NZ = 8
NC = 8
CAP = 3
PAIRS = NB // 2
CHUNK = 4
LANES = 128
TILE = HQ * BLK
NY = 4
NX = 4
NEAR_Z = (2, 6, 1, 7)
OUT_ROWS = ROWS // NY
GROUP_ROWS = HQ * DV
HALF = GROUP_ROWS // 2
PIECE = HALF // 4
NTILE = 256
SCALE2 = DK ** (-0.5) * 1.4426950408889634
MESH = pl.DeviceIdType.MESH
BF16 = jnp.bfloat16
F32 = jnp.float32


def remote(source, target, send_sem, recv_sem, device):
    return pltpu.make_async_remote_copy(
        src_ref=source,
        dst_ref=target,
        send_sem=send_sem,
        recv_sem=recv_sem,
        device_id=device,
        device_id_type=MESH,
    )


def swap_halves(tile):
    return jnp.concatenate([tile[:, 64:], tile[:, :64]], axis=1)


def layer_kernel(
    len_ref,
    id_ref,
    pool_ref,
    gate_ref,
    q_ref,
    suffix_ref,
    prefix_ref,
    w_ref,
    out_ref,
    own,
    plus1,
    plus2,
    plus3,
    minus1,
    minus2,
    minus3,
    far,
    outgoing,
    incoming,
    comp_all,
    near,
    ask_table,
    asked,
    asked_smem,
    place_table,
    place_smem,
    q_raw,
    q_heads,
    gates_all,
    mixed,
    sel_kv,
    w_all,
    heads_out,
    heads_in,
    partial,
    load_sem,
    misc_sem,
    z_send,
    z_recv,
    x_send,
    x_recv,
    comp_send,
    comp_recv,
    ask_send,
    ask_recv,
    ask_load,
    halo_send,
    halo_recv,
    w_send,
    w_recv,
    twin_send,
    twin_recv,
    head_send,
    head_recv,
):
    z = lax.axis_index("sib")
    c = lax.axis_index("ctx")
    y = lax.axis_index("head")

    def z_peer(offset):
        return ((z + offset) % NZ, c, y)

    def c_peer(offset):
        return (z, (c + offset) % NC, y)

    def y_peer(offset):
        return (z, c, (y + offset) % NY)

    core = c % 2
    twin_device = (z, c + 1 - 2 * core, y)

    barrier = pltpu.get_barrier_semaphore()
    for offset in NEAR_Z:
        pl.semaphore_signal(barrier, inc=1, device_id=z_peer(offset), device_id_type=MESH)
    for offset in range(1, NC):
        pl.semaphore_signal(barrier, inc=1, device_id=c_peer(offset), device_id_type=MESH)
    for offset in range(1, NY):
        pl.semaphore_signal(barrier, inc=1, device_id=y_peer(offset), device_id_type=MESH)

    loads = [
        pltpu.make_async_copy(
            prefix_ref.at[:, pl.ds(pair * LANES, LANES)], own.at[pair], load_sem.at[pair]
        )
        for pair in range(PAIRS)
    ]
    for load in loads:
        load.start()
    q_load = pltpu.make_async_copy(q_ref, q_raw, misc_sem.at[0])
    q_load.start()
    near_load = pltpu.make_async_copy(suffix_ref, near.at[:, pl.ds(ROWS, ROWS)], misc_sem.at[1])
    near_load.start()
    w_load = pltpu.make_async_copy(w_ref, w_all.at[0], misc_sem.at[2])
    w_load.start()
    pl.semaphore_wait(barrier, len(NEAR_Z) + NC - 1 + NY - 1)

    def comp_over_z(offset):
        return remote(
            comp_all.at[0, 0],
            comp_all.at[0, NZ - offset],
            comp_send.at[0, offset],
            comp_recv.at[0, NZ - offset],
            z_peer(offset),
        )

    def comp_relay(way):
        return remote(
            comp_all.at[0, (NZ - 2 * way) % NZ],
            comp_all.at[0, (NZ - 3 * way) % NZ],
            comp_send.at[0, 3 if way == 1 else 5],
            comp_recv.at[0, 3 if way == 1 else 5],
            z_peer(way),
        )

    def comp_far(way):
        rows = pl.ds(0 if way == 1 else NB // 2, NB // 2)
        return remote(
            comp_all.at[0, (NZ - 2 * way) % NZ, rows],
            comp_all.at[0, NZ // 2, rows],
            comp_send.at[0, 4 if way == 1 else 0],
            comp_recv.at[0, 4 if way == 1 else 0],
            z_peer(2 * way),
        )

    def comp_over_c(chips):
        return remote(
            comp_all.at[0],
            comp_all.at[NX - chips],
            comp_send.at[1, chips],
            comp_recv.at[1, NX - chips],
            c_peer(2 * chips),
        )

    def comp_to_twin(slot):
        return remote(
            comp_all.at[slot],
            comp_all.at[NX + slot],
            comp_send.at[1, NX + slot],
            comp_recv.at[1, NX + slot],
            twin_device,
        )

    def ask(offset):
        return remote(
            ask_table.at[pl.ds(offset, 1)],
            asked.at[pl.ds(NC - offset, 1)],
            ask_send.at[offset],
            ask_recv.at[NC - offset],
            c_peer(offset),
        )

    def halo():
        return remote(
            suffix_ref, near.at[:, pl.ds(0, ROWS)], halo_send.at[0], halo_recv.at[0], c_peer(1)
        )

    stages = {1: (own, plus1, plus2, plus3, far), -1: (own, minus1, minus2, minus3, far)}

    def z_chunks(way, step):
        if step < 3:
            return tuple(range(4))
        return (0, 1) if way == 1 else (2, 3)

    def z_copy(way, step, chunk):
        row = 0 if way == 1 else 1
        window = pl.ds(CHUNK * chunk, CHUNK)
        return remote(
            stages[way][step].at[window],
            stages[way][step + 1].at[window],
            z_send.at[row, step, chunk],
            z_recv.at[row, step, chunk],
            z_peer(way),
        )

    room = {0: 0, 1: 1, 7: 2, 2: 3, 6: 0, 3: 1, 5: 2, 4: 3}
    room_before = {6: 0, 3: 1, 5: 7, 4: 2}

    def w_copy(way, step, piece):
        row = 0 if way == 1 else 1
        rows = pl.ds(pl.multiple_of(core * HALF + piece * PIECE, PIECE), PIECE)
        near_slot = 3 if way == 1 else 1
        return remote(
            w_ref.at[rows] if step == 0 else w_all.at[near_slot, rows],
            w_all.at[near_slot if step == 0 else 2, rows],
            w_send.at[row, step, piece],
            w_recv.at[row, step, piece],
            y_peer(way),
        )

    def w_pieces(way, step):
        if step == 0:
            return (0, 1, 2, 3) if way == 1 else (2, 3, 0, 1)
        return (0, 1) if way == 1 else (2, 3)

    def twin_copy(slot, piece):
        rows = pl.ds(pl.multiple_of(core * HALF + piece * PIECE, PIECE), PIECE)
        return remote(
            w_all.at[slot, rows],
            w_all.at[slot, rows],
            twin_send.at[slot, piece],
            twin_recv.at[slot, piece],
            twin_device,
        )

    def twin_arrival(slot, piece):
        rows = pl.ds(pl.multiple_of((1 - core) * HALF + piece * PIECE, PIECE), PIECE)
        return remote(
            w_all.at[slot, rows],
            w_all.at[slot, rows],
            twin_send.at[slot, piece],
            twin_recv.at[slot, piece],
            twin_device,
        )

    def w_service(step, turn):
        for way in (1, -1):
            piece = w_pieces(way, step)[turn]
            w_copy(way, step, piece).wait_recv()
            if step == 0 and piece in w_pieces(way, 1):
                w_copy(way, 1, piece).start()
            if step == 0:
                twin_copy(3 if way == 1 else 1, piece).start()

    def w_far_twins(turn):
        for way in (1, -1):
            twin_copy(2, w_pieces(way, 1)[turn]).start()

    def head_copy(offset, part):
        rows = pl.ds(part * BLK, BLK)
        return remote(
            heads_out.at[offset, rows],
            heads_in.at[NY - offset, rows],
            head_send.at[offset, part],
            head_recv.at[NY - offset, part],
            y_peer(offset),
        )

    def x_copy(plane, offset):
        return remote(
            outgoing.at[pl.ds((room[plane] * NC + offset) * CAP, CAP)],
            incoming.at[pl.ds((plane * NC + NC - offset) * CAP, CAP)],
            x_send.at[plane, offset],
            x_recv.at[plane, NC - offset],
            c_peer(offset),
        )

    left_half = lax.broadcasted_iota(jnp.int32, (KV // 2, LANES), 1) < BLK

    planes = {0: own, 7: plus1, 6: plus2, 5: plus3, 1: minus1, 2: minus2, 3: minus3, 4: far}

    def exchange(plane):
        held = planes[plane]
        if plane in room_before:
            for offset in range(1, NC):
                x_copy(room_before[plane], offset).wait_send()

        def peer_at(turn):
            offset = turn * 0
            for index, value in enumerate((4, 5, 3, 2, 6, 7, 1)):
                offset = jnp.where(turn == index, value, offset)
            return offset

        def serve(turn, carry):
            offset = peer_at(turn)
            for slot in range(CAP):
                pair = asked_smem[offset, plane * 8 + slot]
                half = asked_smem[offset, plane * 8 + CAP + slot]
                tile = held[pair]
                upper = tile[: KV // 2]
                lower = tile[KV // 2 :]
                first = half == 0
                kept_upper = jnp.where(first, upper, swap_halves(upper))
                kept_lower = jnp.where(first, swap_halves(lower), lower)
                outgoing[(room[plane] * NC + offset) * CAP + slot] = jnp.where(
                    left_half, kept_upper, kept_lower
                )

            @pl.when(turn >= 1)
            def _():
                x_copy(plane, peer_at(turn - 1)).start()

            return carry

        lax.fori_loop(0, NC, serve, 0)
        incoming[pl.ds(plane * NC * CAP, CAP)] = outgoing[pl.ds(room[plane] * NC * CAP, CAP)]

    def forward(step, chunk):
        for way in (1, -1):
            if chunk in z_chunks(way, step):
                z_copy(way, step, chunk).wait_recv()
                if step < 3 and chunk in z_chunks(way, step + 1):
                    z_copy(way, step + 1, chunk).start()

    nt = (((1,), (1,)), ((), ()))

    halo().start()
    for way in (1, -1):
        w_copy(way, 0, w_pieces(way, 0)[0]).start()
    for load in loads:
        load.wait()
    for chunk in range(3):
        for way in (1, -1):
            z_copy(way, 0, chunk).start()

    ids = jnp.concatenate([id_ref[0, block] for block in range(QB)], axis=1)
    owner = ids // NB
    local = ids % NB
    plane_of = (owner // NC - z + NZ) % NZ
    offset_of = (owner % NC - c + NC) % NC
    place = offset_of * NZ + plane_of
    square = (LANES, LANES)
    down = lax.broadcasted_iota(jnp.int32, square, 0)
    along = lax.broadcasted_iota(jnp.int32, square, 1)
    place_along = jnp.broadcast_to(place, square)
    place_down = jnp.sum(jnp.where(down == along, place_along, 0), axis=1, keepdims=True)
    rank = jnp.sum(
        jnp.where((place_down == place_along) & (down < along), 1, 0), axis=0, keepdims=True
    )
    landing = (plane_of * NC + offset_of) * CAP + jnp.minimum(rank, CAP - 1)
    place_table[...] = jnp.broadcast_to(landing, (8, LANES))
    wide = (NC * NZ, LANES)
    matches = lax.broadcasted_iota(jnp.int32, wide, 0) == place
    lane = lax.broadcasted_iota(jnp.int32, wide, 1)
    table = jnp.zeros(wide, jnp.int32)
    own_lanes = lane // 8 == lax.broadcasted_iota(jnp.int32, wide, 0) % NZ
    for slot in range(CAP):
        hit = matches & (rank == slot)
        pair_value = jnp.sum(jnp.where(hit, local // 2, 0), axis=1, keepdims=True)
        half_value = jnp.sum(jnp.where(hit, local % 2, 0), axis=1, keepdims=True)
        table = jnp.where(own_lanes & (lane % 8 == slot), pair_value, table)
        table = jnp.where(own_lanes & (lane % 8 == CAP + slot), half_value, table)
    ask_table[...] = jnp.sum(table.reshape(NC, NZ, LANES), axis=1)

    rows3 = 3 * NB
    down3 = lax.broadcasted_iota(jnp.int32, (rows3, LANES), 0)
    along3 = lax.broadcasted_iota(jnp.int32, (rows3, LANES), 1)

    def parts_of(row):
        weights = jnp.concatenate([pool_ref[row : row + 1, :]] * 2, axis=1)
        high = weights.astype(BF16).astype(F32)
        middle = (weights - high).astype(BF16).astype(F32)
        low = weights - high - middle
        return jnp.where(down3 < NB, high, jnp.where(down3 < 2 * NB, middle, low))

    key_parts = parts_of(0)
    value_parts = parts_of(1)

    def compress(pair, sums):
        mine = down3 % NB == 2 * pair + along3 // BLK
        tile = own[pair]
        keys = lax.dot_general(
            jnp.where(mine, key_parts, 0.0).astype(BF16),
            tile[:DK],
            nt,
            preferred_element_type=F32,
        )
        values = lax.dot_general(
            jnp.where(mine, value_parts, 0.0).astype(BF16),
            tile[DK:],
            nt,
            preferred_element_type=F32,
        )
        return sums[0] + keys, sums[1] + values

    key_sums, value_sums = lax.fori_loop(
        0, PAIRS, compress, (jnp.zeros((rows3, DK), F32), jnp.zeros((rows3, DV), F32))
    )
    comp_all[0, 0, :, :DK] = (
        key_sums[:NB] + key_sums[NB : 2 * NB] + key_sums[2 * NB :]
    ).astype(BF16)
    comp_all[0, 0, :, DK : 2 * LANES] = jnp.zeros((NB, 2 * LANES - DK), BF16)
    comp_all[0, 0, :, 2 * LANES :] = (
        value_sums[:NB] + value_sums[NB : 2 * NB] + value_sums[2 * NB :]
    ).astype(BF16)

    for offset in range(1, NC):
        ask(offset).start()
    ask_self = pltpu.make_async_copy(
        ask_table.at[pl.ds(0, 1)], asked.at[pl.ds(0, 1)], ask_load.at[0]
    )
    ask_self.start()
    place_copy = pltpu.make_async_copy(place_table, place_smem, misc_sem.at[3])
    place_copy.start()
    gates_all[...] = jax.nn.sigmoid(gate_ref[...]).T
    for offset in NEAR_Z:
        comp_over_z(offset).start()
    for way in (1, -1):
        z_copy(way, 0, 3).start()
    for turn in range(1, 4):
        for way in (1, -1):
            w_copy(way, 0, w_pieces(way, 0)[turn]).start()

    q_load.wait()
    for head in range(HQ):
        q_heads[head] = q_raw[:, head * DK : (head + 1) * DK]

    for offset in range(1, NC):
        ask(NC - offset).wait_recv()
    ask_self.wait()
    ask_all = pltpu.make_async_copy(asked, asked_smem, ask_load.at[1])
    ask_all.start()
    ask_all.wait()
    place_copy.wait()
    exchange(0)

    def queries_of(block):
        rows = pl.ds(pl.multiple_of(block * BLK, BLK), BLK)
        return q_heads[:, rows, :].reshape(TILE, DK)

    def gate_columns(block):
        rows = pl.ds(pl.multiple_of(block * BLK, BLK), BLK)
        return gates_all[rows, :]

    def softmax(scores, previous_max=None):
        top = jnp.max(scores, axis=-1, keepdims=True)
        if previous_max is not None:
            top = jnp.maximum(previous_max, top)
        weights = jnp.exp2(scores * SCALE2 - top * SCALE2)
        return top, weights, jnp.sum(weights, axis=-1, keepdims=True)

    near_load.wait()
    halo().wait_recv()

    def window_block(block, carry):
        start = pl.multiple_of((block // 2) * LANES, LANES)
        span = pl.ds(start, W + LANES)
        scores = jnp.dot(queries_of(block), near[:DK, span], preferred_element_type=F32)
        scores = scores.reshape(HQ, BLK, W + LANES)
        row = lax.broadcasted_iota(jnp.int32, (1, BLK, W + LANES), 1) + (block % 2) * BLK
        lane = lax.broadcasted_iota(jnp.int32, (1, BLK, W + LANES), 2)
        reach = jnp.where(c == 0, ROWS - start, 0)
        visible = (lane > row) & (lane <= row + W) & (lane >= reach)
        scores = jnp.where(visible, scores, -jnp.inf).reshape(TILE, W + LANES)
        _, weights, total = softmax(scores)
        result = lax.dot_general(
            weights.astype(BF16), near[DK:, span], nt, preferred_element_type=F32
        )
        result = result / total
        gates = gate_columns(block)
        for head in range(HQ):
            mixed[block, head * BLK : (head + 1) * BLK, :] = (
                result[head * BLK : (head + 1) * BLK]
                * gates[:, 2 * HQ + head : 2 * HQ + head + 1]
            )
        return carry

    def window_loop(block, carry):
        window_block(block, carry)

        @pl.when(block == 2)
        def _():
            forward(0, 0)

        @pl.when(block == 5)
        def _():
            forward(0, 1)

        return carry

    lax.fori_loop(0, QB, window_loop, 0)

    for offset in NEAR_Z:
        comp_over_z(NZ - offset).wait_recv()
    for way in (1, -1):
        comp_far(way).start()
        comp_relay(way).start()
    forward(0, 2)
    w_service(0, 0)
    forward(0, 3)
    exchange(1)
    exchange(7)
    w_service(0, 1)
    forward(1, 0)
    for way in (1, -1):
        comp_far(way).wait_recv()
        comp_relay(way).wait_recv()
    for chips in (2, 1, 3):
        comp_over_c(chips).start()
    comp_to_twin(0).start()
    forward(1, 1)
    w_service(0, 2)
    forward(1, 2)
    forward(1, 3)
    exchange(2)
    exchange(6)
    for chips in (1, 3, 2):
        comp_over_c(NX - chips).wait_recv()
        comp_to_twin(chips).start()
    w_service(0, 3)
    forward(2, 0)
    for slot in range(NX):
        comp_to_twin(slot).wait_recv()

    half_keys = NZ * NC * NB // 2

    def comp_block(block, carry):
        queries = queries_of(block)
        comp_flat = comp_all.reshape(NZ * NC * NB, 3 * LANES)
        top = None
        for part in range(2):
            keys = pl.ds(part * half_keys, half_keys)
            scores = lax.dot_general(
                queries, comp_flat[keys, :DK], nt, preferred_element_type=F32
            )
            new_top, weights, total = softmax(scores, top)
            result = jnp.dot(
                weights.astype(BF16), comp_flat[keys, 2 * LANES :], preferred_element_type=F32
            )
            if part == 0:
                top, all_total, all_result = new_top, total, result
            else:
                decay = jnp.exp2((top - new_top) * SCALE2)
                all_total = all_total * decay + total
                all_result = all_result * decay + result
        result = all_result / all_total
        gates = gate_columns(block)
        for head in range(HQ):
            rows = slice(head * BLK, (head + 1) * BLK)
            mixed[block, rows, :] += result[rows] * gates[:, head : head + 1]
        return carry

    def comp_loop(block, carry):
        comp_block(block, carry)

        @pl.when(block == 0)
        def _():
            forward(2, 1)
            w_service(1, 0)
            w_far_twins(0)

        @pl.when(block == 4)
        def _():
            forward(2, 2)

        return carry

    lax.fori_loop(0, QB, comp_loop, 0)

    forward(2, 3)
    exchange(3)
    exchange(5)
    forward(3, 0)
    forward(3, 2)
    w_service(1, 1)
    forward(3, 1)
    forward(3, 3)
    exchange(4)
    w_load.wait()
    w_far_twins(1)
    for plane in (0, 1, 7, 2, 6, 3, 5, 4):
        for offset in range(1, NC):
            x_copy(plane, NC - offset).wait_recv()

    def selected_block(turn, carry):
        group = turn // 2
        target = jnp.where(group == 0, 2, jnp.where(group == 1, 3, jnp.where(group == 2, 1, 0)))
        block = 2 * ((y + target) % NY) + turn % 2
        for pair in range(TOPK // 2):
            first = incoming[place_smem[0, block * TOPK + 2 * pair]]
            second = incoming[place_smem[0, block * TOPK + 2 * pair + 1]]
            lanes = slice(pair * LANES, (pair + 1) * LANES)
            sel_kv[: KV // 2, lanes] = jnp.where(left_half, first, swap_halves(second))
            sel_kv[KV // 2 :, lanes] = jnp.where(left_half, swap_halves(first), second)
        for done in range(QB - 2):

            @pl.when(turn == done + 1)
            def _():
                head_copy((2, 3, 1)[done // 2], done % 2).start()

        scores = jnp.dot(queries_of(block), sel_kv[:DK, :], preferred_element_type=F32)
        _, weights, total = softmax(scores)
        result = lax.dot_general(
            weights.astype(BF16), sel_kv[DK:, :], nt, preferred_element_type=F32
        )
        result = result / total
        gates = gate_columns(block)
        first_row = pl.multiple_of((turn % 2) * BLK, BLK)
        inside = (
            lax.broadcasted_iota(jnp.int32, (BLK, DV), 0) + c * ROWS + block * BLK < len_ref[0]
        )
        for head in range(HQ):
            rows = slice(head * BLK, (head + 1) * BLK)
            value = (
                mixed[block, rows, :] + result[rows] * gates[:, HQ + head : HQ + head + 1]
            )
            heads_out[target, pl.ds(first_row, BLK), head * DV : (head + 1) * DV] = jnp.where(
                inside, value, 0.0
            ).astype(BF16)
        return carry

    lax.fori_loop(0, QB, selected_block, 0)

    for slot in range(1, NY):
        for piece in range(4):
            twin_arrival(slot, piece).wait_recv()
    for part in range(2):
        head_copy(2, part).wait_recv()

    def project_near(index, carry):
        columns = pl.ds(pl.multiple_of(index * NTILE, NTILE), NTILE)
        total = jnp.dot(heads_out[0], w_all[0, :, columns], preferred_element_type=F32)
        total += jnp.dot(heads_in[2], w_all[2, :, columns], preferred_element_type=F32)
        partial[:, columns] = total
        return carry

    lax.fori_loop(0, DM // NTILE, project_near, 0)
    for part in range(2):
        head_copy(3, part).wait_recv()

    def project_next(index, carry):
        columns = pl.ds(pl.multiple_of(index * NTILE, NTILE), NTILE)
        partial[:, columns] += jnp.dot(
            heads_in[1], w_all[1, :, columns], preferred_element_type=F32
        )
        return carry

    lax.fori_loop(0, DM // NTILE, project_next, 0)
    for part in range(2):
        head_copy(1, part).wait_recv()

    def project_last(index, carry):
        columns = pl.ds(pl.multiple_of(index * NTILE, NTILE), NTILE)
        total = jnp.dot(heads_in[3], w_all[3, :, columns], preferred_element_type=F32)
        out_ref[:, columns] = (partial[:, columns] + total).astype(BF16)
        return carry

    lax.fori_loop(0, DM // NTILE, project_last, 0)

    for offset in NEAR_Z:
        comp_over_z(offset).wait_send()
    for way in (1, -1):
        comp_far(way).wait_send()
        comp_relay(way).wait_send()
    for offset in range(1, NC):
        ask(offset).wait_send()
        for plane in (6, 3, 5, 4):
            x_copy(plane, offset).wait_send()
    halo().wait_send()
    for chips in range(1, NX):
        comp_over_c(chips).wait_send()
    for slot in range(NX):
        comp_to_twin(slot).wait_send()
    for way in (1, -1):
        for step in range(2):
            for piece in w_pieces(way, step):
                w_copy(way, step, piece).wait_send()
    for slot in range(1, NY):
        for part in range(2):
            head_copy(slot, part).wait_send()
        for piece in range(4):
            twin_copy(slot, piece).wait_send()
    for step in range(4):
        for way in (1, -1):
            for chunk in z_chunks(way, step):
                z_copy(way, step, chunk).wait_send()


def shards(queries, suffix_kv, prefix_kv, pooling, gate_logits, selected, lengths, w_out):
    anywhere = pl.BlockSpec(memory_space=pl.ANY)
    vmem = pl.BlockSpec(memory_space=pltpu.VMEM)
    smem = pl.BlockSpec(memory_space=pltpu.SMEM)
    plane = pltpu.VMEM((PAIRS, KV, LANES), BF16)
    dma = pltpu.SemaphoreType.DMA
    out = pl.pallas_call(
        layer_kernel,
        name="layer",
        out_shape=jax.ShapeDtypeStruct((OUT_ROWS, DM), BF16),
        in_specs=[smem, vmem, vmem, vmem, anywhere, anywhere, anywhere, anywhere],
        out_specs=vmem,
        scratch_shapes=[plane] * 8
        + [
            pltpu.VMEM((4 * NC * CAP, KV // 2, LANES), BF16),
            pltpu.VMEM((NZ * NC * CAP, KV // 2, LANES), BF16),
            pltpu.VMEM((NC, NZ, NB, 3 * LANES), BF16),
            pltpu.VMEM((KV, 2 * ROWS), BF16),
            pltpu.VMEM((NC, LANES), jnp.int32),
            pltpu.VMEM((NC, LANES), jnp.int32),
            pltpu.SMEM((NC, LANES), jnp.int32),
            pltpu.VMEM((8, LANES), jnp.int32),
            pltpu.SMEM((8, LANES), jnp.int32),
            pltpu.VMEM((ROWS, HQ * DK), BF16),
            pltpu.VMEM((HQ, ROWS, DK), BF16),
            pltpu.VMEM((ROWS, 3 * HQ), F32),
            pltpu.VMEM((QB, TILE, DV), F32),
            pltpu.VMEM((KV, TOPK * BLK), BF16),
            pltpu.VMEM((NY, GROUP_ROWS, DM), BF16),
            pltpu.VMEM((NY, OUT_ROWS, GROUP_ROWS), BF16),
            pltpu.VMEM((NY, OUT_ROWS, GROUP_ROWS), BF16),
            pltpu.VMEM((OUT_ROWS, DM), F32),
            dma((PAIRS,)),
            dma((4,)),
            dma((2, 4, 4)),
            dma((2, 4, 4)),
            dma((NZ, NC)),
            dma((NZ, NC)),
            dma((2, NC)),
            dma((2, NC)),
            dma((NC,)),
            dma((NC,)),
            dma((2,)),
            dma((1,)),
            dma((1,)),
            dma((2, 2, 4)),
            dma((2, 2, 4)),
            dma((NY, 4)),
            dma((NY, 4)),
            dma((NY, 2)),
            dma((NY, 2)),
        ],
        compiler_params=pltpu.CompilerParams(
            collective_id=0, has_side_effects=True, vmem_limit_bytes=67_043_328
        ),
    )(
        lengths,
        selected,
        pooling,
        gate_logits.reshape(ROWS, 3 * HQ).T,
        queries.reshape(ROWS, HQ * DK),
        suffix_kv.reshape(ROWS, KV).T,
        prefix_kv.reshape(NB * BLK, KV).T,
        w_out,
    )
    return out.reshape(1, OUT_ROWS, DM)


def solution(mesh):
    return jax.shard_map(
        shards,
        mesh=mesh,
        in_specs=(
            P("sib", "ctx", "head", None),
            P("sib", "ctx", "head", None),
            P(("sib", "ctx"), "head", None),
            P(),
            P("sib", "ctx", "head", None),
            P("sib", "ctx", "head", None),
            P("sib"),
            P("head", None),
        ),
        out_specs=P("sib", ("ctx", "head"), None),
        check_vma=False,
    )
```
